512 devices in a mesh: row: 32 (over y, z_lo, core), col: 16 (over x, z_hi).
Axes of the slice: x: 4, y: 8, z: 8 (z_hi: 4, z_lo: 2; z = z_hi * 2 + z_lo), core: 2. Of those that a mesh axis runs over, the one named last changes fastest.
Arguments:
- features: bfloat16 [32768, 256], P(('row', 'col')), may hold values from -6 to 6
- grad_out: bfloat16 [32768, 256], P(('row', 'col')), may hold values from -6 to 6
- relu_mask: int32 [32768, 256], P(('row', 'col')), may hold values 0 or 1
- degree: int32 [32768], P(('row', 'col')), may hold values from 1 to 16
- weight: bfloat16 [256, 256], replicated, may hold values from -0.375 to 0.375
- adjacency: bfloat16 [32, 16, 96, 128, 128], P('row', 'col'), may hold values from -0.0625 to 0.0625
- block_slot: int32 [32, 16, 96], P('row', 'col'), may hold values from 0 to 127, as said below
- block_count: int32 [32, 16], P('row', 'col'), may hold values from 1 to 96, as said below
Outputs:
- grad_features: float32 [32768, 256], P(('row', 'col'))
- weight_grad: float32 [256, 256], replicated
The draws below stay inside these ranges and needn't reach their ends.
Inputs may be any that keep to these rules, and one draw needn't show every extreme that they name: `block_slot`: within one tile the positions are distinct. `block_count`: some tile uses all 96 entries.
All inputs are finite; a program needn't handle non-finite values. No bound on the sum of `relu_mask` on one device may be relied on, other than what follows from the above.
Results may differ from the reference program's by a relative error of at most 0.0075.
Values may be sent and summed in bfloat16 or wider, within the bound.
A program may use at most 64 MiB of HBM per device.

```python
import jax
import jax.numpy as jnp
from jax import lax

F = 256
BLK = 128
ROWS_DEV = 64
NODES = 32768
TILE_ROWS = 1024
TILE_COLS = 2048
SLOTS = 128
MAXB = 96
N_ROW = 32
N_COL = 16


def draw_block_slot(key, part):
    tile_keys = jax.random.split(key, N_ROW * N_COL)
    orders = jax.vmap(lambda k: jax.random.permutation(k, SLOTS)[:MAXB])(tile_keys)
    return orders.reshape(N_ROW, N_COL, MAXB).astype(jnp.int32)


def draw_block_count(key, part):
    uniform_ints = jax.random.randint(key, (N_ROW * N_COL,), 0, MAXB + 1)
    skewed = jnp.maximum(1, uniform_ints * uniform_ints // MAXB)
    chosen = jax.random.randint(jax.random.fold_in(key, 7), (), 0, N_ROW * N_COL)
    filled = jnp.where(jnp.arange(N_ROW * N_COL) == chosen, MAXB, skewed)
    return filled.reshape(N_ROW, N_COL).astype(jnp.int32)


def plant(array, rng, low, high):
    longest = array.shape.index(max(array.shape))
    spots = []
    for shift in (0, 1):
        where = [jax.random.randint(jax.random.fold_in(rng, axis), (), 0, length) for axis, length in enumerate(array.shape)]
        where[longest] = (where[longest] + shift) % array.shape[longest]
        spots.append(tuple(where))
    return array.at[spots[0]].set(low).at[spots[1]].set(high)


def block_scale(key, extent, cuts, low, high):
    level, own = 1.0, jax.random.fold_in(key, 6)
    for position, shards_of in cuts:
        steps = jnp.exp(jax.random.uniform(jax.random.fold_in(own, position), (shards_of,), jnp.float32, low / len(cuts), high / len(cuts)))
        level = level * jnp.repeat(steps, extent[position] // shards_of).reshape([-1 if axis == position else 1 for axis in range(len(extent))])
    return level


def normal_values(key, dims, spread, limit, cuts=(), dtype=jnp.bfloat16):
    array = jax.random.normal(key, dims, jnp.float32) * spread
    if len(cuts) > 0:
        array = block_scale(key, dims, cuts, -0.22, 0.18) * array
    return jnp.clip(array, min=-limit, max=limit).astype(dtype)


def setup_inputs(seed: int = 0) -> dict:
    splits = jax.random.split(jax.random.key(seed), 9)
    features = normal_values(splits[0], (NODES, F), 1.0, 6.0, ((0, 512),))
    grad_out = normal_values(splits[1], (NODES, F), 1.0, 6.0, ((0, 512),))
    relu_mask = plant((jax.random.randint(splits[2], (NODES, F), 0, 2) < 1).astype(jnp.int32), jax.random.fold_in(splits[2], 1), 0, 1)
    degree = plant(jax.random.randint(splits[3], (NODES,), 1, 17), jax.random.fold_in(splits[3], 1), 1, 16).astype(jnp.int32)
    weight = normal_values(splits[4], (F, F), F ** -0.5, 0.375)
    adjacency = normal_values(splits[5], (N_ROW, N_COL, MAXB, BLK, BLK), (max(BLK, BLK * MAXB * N_ROW // (3 * (TILE_COLS // BLK)))) ** -0.5, 0.0625, ((0, 32), (1, 16)))
    block_slot = draw_block_slot(jax.random.fold_in(splits[8], 71), 0)
    block_count = draw_block_count(jax.random.fold_in(splits[8], 71), 0)
    return {"features": features, "grad_out": grad_out, "relu_mask": relu_mask, "degree": degree, "weight": weight, "adjacency": adjacency, "block_slot": block_slot, "block_count": block_count}


def tile_pass(blocks, slots, live_count, source, transpose):
    col_blocks = TILE_COLS // BLK
    row_blocks = TILE_ROWS // BLK
    block_row = slots // col_blocks
    block_col = slots % col_blocks
    live_mask = (jnp.arange(MAXB) < live_count).astype(jnp.float32)
    pieces = source.reshape(-1, BLK, F).astype(jnp.float32)
    tiles_f = blocks.astype(jnp.float32)
    if transpose:
        picked = pieces[block_row]
        products = jnp.einsum('gab,gaf->gbf', tiles_f, picked, precision=lax.Precision.HIGHEST)
        products = products * live_mask[:, None, None]
        return jnp.zeros((col_blocks, BLK, F), jnp.float32).at[block_col].add(products).reshape(TILE_COLS, F)
    picked = pieces[block_col]
    products = jnp.einsum('gab,gbf->gaf', tiles_f, picked, precision=lax.Precision.HIGHEST)
    products = products * live_mask[:, None, None]
    return jnp.zeros((row_blocks, BLK, F), jnp.float32).at[block_row].add(products).reshape(TILE_ROWS, F)

def reference(features, grad_out, relu_mask, degree, weight, adjacency, block_slot, block_count):
    node_scale = lax.rsqrt(degree.astype(jnp.float32))[:, None]
    masked = grad_out * relu_mask.astype(jnp.bfloat16)
    scaled_grad = (masked.astype(jnp.float32) * node_scale).astype(jnp.bfloat16)
    scaled_feat = (features.astype(jnp.float32) * node_scale).astype(jnp.bfloat16)
    grad_rows = scaled_grad.reshape(N_ROW, TILE_ROWS, F)
    feat_cols = scaled_feat.reshape(N_ROW, N_COL, ROWS_DEV, F).transpose(1, 0, 2, 3).reshape(N_COL, TILE_COLS, F)

    def over_row(running, row_index):
        blocks = adjacency[row_index]
        slots = block_slot[row_index]
        counts = block_count[row_index]
        back = jax.vmap(lambda b, s, c: tile_pass(b, s, c, grad_rows[row_index], True))(blocks, slots, counts)
        ahead = jax.vmap(lambda b, s, c, x: tile_pass(b, s, c, x, False))(blocks, slots, counts, feat_cols)
        return (running + back, lax.optimization_barrier(jnp.sum(ahead, axis=0)))
    col_total, row_total = lax.scan(over_row, jnp.zeros((N_COL, TILE_COLS, F), jnp.float32), jnp.arange(N_ROW))
    pulled = col_total.reshape(N_COL, N_ROW, ROWS_DEV, F).transpose(1, 0, 2, 3).reshape(NODES, F) * node_scale
    aggregated = row_total.reshape(NODES, F) * node_scale
    grad_features = jnp.dot(pulled, weight.astype(jnp.float32).T, precision=lax.Precision.HIGHEST)
    weight_grad = jnp.dot(aggregated.T, masked.astype(jnp.float32), precision=lax.Precision.HIGHEST) * NODES ** (-0.5)
    return (grad_features, weight_grad)
```

```python
import functools

import jax
import jax.numpy as jnp
from jax import lax
from jax.experimental import pallas as pl
from jax.experimental.pallas import tpu as pltpu
from jax.sharding import PartitionSpec as P

MESH = pl.DeviceIdType.MESH
BF = jnp.bfloat16
F32 = jnp.float32


def kernel(
    R, C, norm,
    feat_ref, gout_ref, mask_ref, deg_ref, w_ref, adj_hbm, slot_ref, count_ref,
    gf_ref, wg_ref,
    adj_v, a_dense, inv_v, inv_s, gbuf, gt, pall,
    s1_send, s1_recv, s2_send, s2_recv, s3_send, s3_recv, own,
    wpart, ra, wb, rb, rc,
    adj_sem, inv_sem, g_ss, g_rs, s1_ss, s1_rs, s2_ss, s2_rs, s3_ss, s3_rs,
    a_ss, a_rs, b_ss, b_rs, c_ss, c_rs, d_ss, d_rs, e_ss, e_rs,
):
    NY = R // 4
    M = R // 2
    entries, blk = adj_hbm.shape[0], adj_hbm.shape[1]
    width = feat_ref.shape[1]
    row = lax.axis_index("row")
    col = lax.axis_index("col")
    y = row // 4
    z = (row // 2) % 2
    c = row % 2
    m = row // 2
    sib = m * 2 + (1 - c)
    zrow = y * 4 + (1 - z) * 2 + c

    def rcopy(src, dst, ss, rs, dev):
        return pltpu.make_async_remote_copy(
            src_ref=src, dst_ref=dst, send_sem=ss, recv_sem=rs,
            device_id=dev, device_id_type=MESH,
        )

    adj_copy = pltpu.make_async_copy(adj_hbm, adj_v.at[pl.ds(0, entries)], adj_sem)
    adj_copy.start()

    bar = pltpu.get_barrier_semaphore()

    def greet_col(t, u):
        pl.semaphore_signal(bar, inc=1, device_id=(row, (col + t) % C), device_id_type=MESH)
        return u

    def greet_row(t, u):
        pl.semaphore_signal(bar, inc=1, device_id=(((m + t) % M) * 2 + c, col), device_id_type=MESH)
        return u

    lax.fori_loop(1, C, greet_col, 0)
    lax.fori_loop(1, M, greet_row, 0)
    pl.semaphore_signal(bar, inc=1, device_id=(sib, col), device_id_type=MESH)

    n = feat_ref.shape[0]
    scale_row = lax.rsqrt(deg_ref[...].astype(F32))
    eye = lax.broadcasted_iota(jnp.int32, (n, n), 0) == lax.broadcasted_iota(jnp.int32, (n, n), 1)
    scale = jnp.sum(jnp.where(eye, jnp.broadcast_to(scale_row, (n, n)), 0.0), axis=1, keepdims=True)
    masked = gout_ref[...].astype(F32) * mask_ref[...].astype(F32)
    gbuf[col] = (masked * scale).astype(BF)

    pl.semaphore_wait(bar, C - 1 + M - 1 + 1)

    def g_send(t, u):
        peer = (col + t) % C
        rcopy(gbuf.at[col], gbuf.at[col], g_ss.at[t], g_rs.at[col], (row, peer)).start()
        return u

    lax.fori_loop(1, C, g_send, 0)

    lane = lax.broadcasted_iota(jnp.int32, (8, 128), 1)
    live = count_ref[0, 0]

    def invert(b, acc):
        s = jnp.where(b < live, slot_ref[0, b], -1)
        return jnp.where(lane == s, b, acc)

    inv_v[...] = lax.fori_loop(0, entries, invert, jnp.full((8, 128), entries, jnp.int32))
    inv_copy = pltpu.make_async_copy(inv_v, inv_s, inv_sem)
    inv_copy.start()
    adj_v[entries] = jnp.zeros((blk, blk), BF)
    inv_copy.wait()
    adj_copy.wait()

    row_blocks = C * n // blk

    def fill(k, u):
        r = k // NY
        q = k % NY
        for h in range(2):
            e = inv_s[0, r * (2 * NY) + q * 2 + h]
            a_dense[q, pl.ds(pl.multiple_of(r * blk, blk), blk), pl.ds(h * blk, blk)] = adj_v[e]
        return u

    lax.fori_loop(0, row_blocks * NY, fill, 0)

    def g_wait(t, u):
        peer = (col + t) % C
        rcopy(gbuf.at[peer], gbuf.at[peer], g_ss.at[t], g_rs.at[peer], (row, peer)).wait()
        return u

    lax.fori_loop(1, C, g_wait, 0)

    def turn(k, u):
        piece = gbuf[pl.ds(2 * k, 2)].reshape(2 * n, width).astype(F32)
        gt[k] = piece.T.astype(BF)
        return u

    lax.fori_loop(0, C // 2, turn, 0)
    gtv = jnp.concatenate([gt[k] for k in range(C // 2)], axis=1)

    def product(t, u):
        q = (y + 1 + t) % NY
        pt = jnp.dot(gtv, a_dense[q], preferred_element_type=F32)
        pall[q] = pt.T.reshape(4, n, width)
        for zz in range(2):
            s1_send[q, zz] = pall[q, 2 * zz + 1 - c].astype(BF)
        rcopy(s1_send.at[q], s1_recv.at[q], s1_ss.at[q], s1_rs.at[q], (sib, col)).start()
        return u

    lax.fori_loop(0, NY, product, 0)

    def stage2(t, u):
        q = (y + 1 + t) % NY
        rcopy(s1_send.at[q], s1_recv.at[q], s1_ss.at[q], s1_rs.at[q], (sib, col)).wait()
        s2_send[q] = (pall[q, 2 * (1 - z) + c] + s1_recv[q, 1 - z].astype(F32)).astype(BF)
        rcopy(s2_send.at[q], s2_recv.at[q], s2_ss.at[q], s2_rs.at[q], (zrow, col)).start()
        return u

    lax.fori_loop(0, NY, stage2, 0)

    def total3(q):
        rcopy(s2_send.at[q], s2_recv.at[q], s2_ss.at[q], s2_rs.at[q], (zrow, col)).wait()
        return pall[q, 2 * z + c] + s1_recv[q, z].astype(F32) + s2_recv[q].astype(F32)

    def stage3(t, u):
        q = (y + 1 + t) % NY
        s3_send[q] = total3(q).astype(BF)
        rcopy(s3_send.at[q], s3_recv.at[y], s3_ss.at[q], s3_rs.at[y], (q * 4 + z * 2 + c, col)).start()
        return u

    lax.fori_loop(0, NY - 1, stage3, 0)
    own[...] = total3(y)

    def collect(t, u):
        q = (y + 1 + t) % NY
        rcopy(s3_send.at[q], s3_recv.at[q], s3_ss.at[q], s3_rs.at[q], (q * 4 + z * 2 + c, col)).wait()
        own[...] += s3_recv[q].astype(F32)
        return u

    lax.fori_loop(0, NY - 1, collect, 0)

    raw = own[...]
    sfeat = (feat_ref[...].astype(F32) * scale).astype(BF)
    raw_hi = raw.astype(BF)
    raw_lo = (raw - raw_hi.astype(F32)).astype(BF)
    over_nodes = (((0,), (0,)), ((), ()))
    wl = lax.dot_general(sfeat, raw_hi, over_nodes, preferred_element_type=F32)
    wl = wl + lax.dot_general(sfeat, raw_lo, over_nodes, preferred_element_type=F32)
    wpart[...] = wl.reshape(wpart.shape)

    rcopy(wpart.at[1 - c], ra, a_ss, a_rs, (sib, col)).start()

    pulled = raw * scale
    p_hi = pulled.astype(BF)
    p_lo = (pulled - p_hi.astype(F32)).astype(BF)
    over_last = (((1,), (1,)), ((), ()))
    w = w_ref[...]
    gf_ref[...] = lax.dot_general(p_hi, w, over_last, preferred_element_type=F32) + lax.dot_general(
        p_lo, w, over_last, preferred_element_type=F32
    )

    rcopy(wpart.at[1 - c], ra, a_ss, a_rs, (sib, col)).wait()
    wb[...] = wpart[c] + ra[...]

    def b_send(t, u):
        peer = (m + t) % M
        rcopy(wb.at[peer], rb.at[m], b_ss.at[t], b_rs.at[m], (peer * 2 + c, col)).start()
        return u

    lax.fori_loop(1, M, b_send, 0)
    rb[m] = wb[m]

    def b_wait(t, u):
        peer = (m + t) % M
        rcopy(wb.at[peer], rb.at[peer], b_ss.at[t], b_rs.at[peer], (peer * 2 + c, col)).wait()
        return u

    lax.fori_loop(1, M, b_wait, 0)
    rc[col] = jnp.sum(rb[...], axis=0)

    def c_send(t, u):
        peer = (col + t) % C
        rcopy(rc.at[col], rc.at[col], c_ss.at[t], c_rs.at[col], (row, peer)).start()
        return u

    lax.fori_loop(1, C, c_send, 0)

    def c_wait(t, u):
        peer = (col + t) % C
        rcopy(rc.at[peer], rc.at[peer], c_ss.at[t], c_rs.at[peer], (row, peer)).wait()
        return u

    lax.fori_loop(1, C, c_wait, 0)
    wg_ref[c, m] = jnp.sum(rc[...], axis=0) * norm

    def d_send(t, u):
        peer = (m + t) % M
        rcopy(wg_ref.at[c, m], wg_ref.at[c, m], d_ss.at[t], d_rs.at[m], (peer * 2 + c, col)).start()
        return u

    lax.fori_loop(1, M, d_send, 0)

    def d_wait(t, u):
        peer = (m + t) % M
        rcopy(wg_ref.at[c, peer], wg_ref.at[c, peer], d_ss.at[t], d_rs.at[peer], (peer * 2 + c, col)).wait()
        return u

    lax.fori_loop(1, M, d_wait, 0)
    rcopy(wg_ref.at[c], wg_ref.at[c], e_ss, e_rs, (sib, col)).start()
    rcopy(wg_ref.at[1 - c], wg_ref.at[1 - c], e_ss, e_rs, (sib, col)).wait()


def local(features, grad_out, relu_mask, degree, weight, adjacency, block_slot, block_count):
    R = lax.axis_size("row")
    C = lax.axis_size("col")
    n, width = features.shape
    entries, blk = adjacency.shape[2], adjacency.shape[3]
    NY, M = R // 4, R // 2
    part = (2, M, width // R, width)
    dma = pltpu.SemaphoreType.DMA
    vm = pltpu.VMEM
    vspec = pl.BlockSpec(memory_space=pltpu.VMEM)
    sspec = pl.BlockSpec(memory_space=pltpu.SMEM)
    gf, wg = pl.pallas_call(
        functools.partial(kernel, R, C, float((n * R * C) ** -0.5)),
        out_shape=(
            jax.ShapeDtypeStruct((n, width), F32),
            jax.ShapeDtypeStruct(part, F32),
        ),
        in_specs=[vspec] * 5 + [pl.BlockSpec(memory_space=pl.ANY), sspec, sspec],
        out_specs=(vspec, vspec),
        scratch_shapes=[
            vm((entries + 1, blk, blk), BF),
            vm((NY, C * n, 2 * blk), BF),
            vm((8, 128), jnp.int32),
            pltpu.SMEM((8, 128), jnp.int32),
            vm((C, n, width), BF),
            vm((C // 2, width, 2 * n), BF),
            vm((NY, 4, n, width), F32),
            vm((NY, 2, n, width), BF),
            vm((NY, 2, n, width), BF),
            vm((NY, n, width), BF),
            vm((NY, n, width), BF),
            vm((NY, n, width), BF),
            vm((NY, n, width), BF),
            vm((n, width), F32),
            vm(part, F32),
            vm(part[1:], F32),
            vm(part[1:], F32),
            vm(part[1:], F32),
            vm((C,) + part[2:], F32),
            dma, dma,
            dma((C,)), dma((C,)),
            dma((NY,)), dma((NY,)),
            dma((NY,)), dma((NY,)),
            dma((NY,)), dma((NY,)),
            dma, dma,
            dma((M,)), dma((M,)),
            dma((C,)), dma((C,)),
            dma((M,)), dma((M,)),
            dma, dma,
        ],
        compiler_params=pltpu.CompilerParams(
            collective_id=0, has_side_effects=True, vmem_limit_bytes=56 * 1024 * 1024
        ),
    )(
        features, grad_out, relu_mask, degree.reshape(1, n), weight,
        adjacency.reshape(entries, blk, blk), block_slot.reshape(1, entries), block_count,
    )
    return gf, wg.reshape(width, width)


def solution(mesh):
    placed = (
        P(("row", "col"), None),
        P(("row", "col"), None),
        P(("row", "col"), None),
        P(("row", "col")),
        P(),
        P("row", "col", None, None, None),
        P("row", "col", None),
        P("row", "col"),
    )
    return jax.shard_map(
        local, mesh=mesh, in_specs=placed, out_specs=(P(("row", "col"), None), P()), check_vma=False
    )
```

```python
import functools

import jax
import jax.numpy as jnp
from jax import lax
from jax.experimental import pallas as pl
from jax.experimental.pallas import tpu as pltpu
from jax.sharding import PartitionSpec as P

MESH = pl.DeviceIdType.MESH
BF = jnp.bfloat16
F32 = jnp.float32


def kernel(
    R, C, ZH, norm,
    feat_hbm, gout_hbm, mask_hbm, deg_hbm, w_hbm, adj_hbm, slot_ref, count_ref,
    gf_ref, wg_ref,
    feat_v, gout_v, mask_v, deg_v, w_v,
    adj_v, a_dense, inv_v, inv_s, gbuf, fbuf, gt, ptb, pall,
    s1_recv, s2_send, s2_recv, s3_send, s3_recv, own,
    wpart, ra, wb, rb, rc,
    in_sem, adj_sem, inv_sem, gz_ss, gx_ss, g_rs, fy_ss, fz_ss, fc_ss, f_rs,
    s1_ss, s1_rs, s2_ss, s2_rs, s3_ss, s3_rs,
    a_ss, a_rs, b_ss, b_rs, c_ss, c_rs, d_ss, d_rs, e_ss, e_rs,
):
    NY = R // 4
    M = R // 2
    X = C // ZH
    entries, blk = adj_hbm.shape[0], adj_hbm.shape[1]
    n, width = feat_hbm.shape
    row = lax.axis_index("row")
    col = lax.axis_index("col")
    y = row // 4
    z = (row // 2) % 2
    c = row % 2
    m = row // 2
    x = col // ZH
    zh = col % ZH
    sib = (m * 2 + (1 - c), col)
    zdev = (y * 4 + (1 - z) * 2 + c, col)

    def ydev(k):
        return (k * 4 + z * 2 + c, col)

    def rcopy(src, dst, ss, rs, dev):
        return pltpu.make_async_remote_copy(
            src_ref=src, dst_ref=dst, send_sem=ss, recv_sem=rs,
            device_id=dev, device_id_type=MESH,
        )

    def each(lo, hi, body):
        def step(t, u):
            body(t)
            return u

        lax.fori_loop(lo, hi, step, 0)

    loads = [
        pltpu.make_async_copy(s, d, in_sem.at[k])
        for k, (s, d) in enumerate(
            [(gout_hbm, gout_v), (mask_hbm, mask_v), (deg_hbm, deg_v), (feat_hbm, feat_v), (w_hbm, w_v)]
        )
    ]
    for copy in loads:
        copy.start()
    adj_copy = pltpu.make_async_copy(adj_hbm, adj_v.at[pl.ds(0, entries)], adj_sem)
    adj_copy.start()

    bar = pltpu.get_barrier_semaphore()

    def greet(dev):
        pl.semaphore_signal(bar, inc=1, device_id=dev, device_id_type=MESH)

    each(1, ZH, lambda t: greet((row, x * ZH + (zh + t) % ZH)))
    each(1, X, lambda t: greet((row, ((x + t) % X) * ZH + zh)))
    each(1, NY, lambda t: greet(ydev((y + t) % NY)))
    greet(zdev)
    greet(sib)

    for copy in loads[:3]:
        copy.wait()
    scale_row = lax.rsqrt(deg_v[...].astype(F32))
    eye = lax.broadcasted_iota(jnp.int32, (n, n), 0) == lax.broadcasted_iota(jnp.int32, (n, n), 1)
    scale = jnp.sum(jnp.where(eye, jnp.broadcast_to(scale_row, (n, n)), 0.0), axis=1, keepdims=True)
    masked = gout_v[...].astype(F32) * mask_v[...].astype(F32)
    gbuf[col] = (masked * scale).astype(BF)
    loads[3].wait()
    fbuf[row] = (feat_v[...].astype(F32) * scale).astype(BF)

    pl.semaphore_wait(bar, ZH - 1 + X - 1 + NY - 1 + 2)

    def g_copy(slot, ss, dev):
        return rcopy(gbuf.at[slot], gbuf.at[slot], ss, g_rs.at[slot], dev)

    def f_copy(slot, ss, dev):
        return rcopy(fbuf.at[slot], fbuf.at[slot], ss, f_rs.at[slot], dev)

    def to_z(t):
        return g_copy(col, gz_ss.at[t], (row, x * ZH + (zh + t) % ZH))

    def to_x(k, t):
        return g_copy(x * ZH + (zh + k) % ZH, gx_ss.at[k, t], (row, ((x + t) % X) * ZH + zh))

    def f_to_y(t):
        return f_copy(row, fy_ss.at[t], ydev((y + t) % NY))

    def f_to_z(k):
        return f_copy(k * 4 + z * 2 + c, fz_ss.at[k], zdev)

    def f_to_sib(k, zz):
        return f_copy(k * 4 + zz * 2 + c, fc_ss.at[k, zz], sib)

    each(1, ZH, lambda t: to_z(t).start())
    each(1, NY, lambda t: f_to_y(t).start())
    each(1, X, lambda t: to_x(0, t).start())
    f_to_z(y).start()
    f_to_sib(y, z).start()

    lane = lax.broadcasted_iota(jnp.int32, (8, 128), 1)
    live = count_ref[0, 0]

    def invert(b, acc):
        s = jnp.where(b < live, slot_ref[0, b], -1)
        return jnp.where(lane == s, b, acc)

    inv_v[...] = lax.fori_loop(0, entries, invert, jnp.full((8, 128), entries, jnp.int32))
    inv_copy = pltpu.make_async_copy(inv_v, inv_s, inv_sem)
    inv_copy.start()
    adj_v[entries] = jnp.zeros((blk, blk), BF)
    inv_copy.wait()
    adj_copy.wait()

    def fill(k):
        r = k // NY
        q = k % NY
        for h in range(2):
            e = inv_s[0, r * (2 * NY) + q * 2 + h]
            a_dense[q, pl.ds(pl.multiple_of(r * blk, blk), blk), pl.ds(h * blk, blk)] = adj_v[e]

    each(0, C * n // blk * NY, fill)

    def forward_x(k):
        slot = x * ZH + (zh + k) % ZH
        g_copy(slot, gz_ss.at[k], sib).wait_recv()
        each(1, X, lambda t: to_x(k, t).start())

    for k in sorted(range(1, ZH), key=lambda k: min(k, ZH - k)):
        forward_x(k)

    def forward_y(t):
        k = (y + t) % NY
        f_copy(k * 4 + z * 2 + c, fz_ss.at[k], sib).wait_recv()
        f_to_z(k).start()
        f_to_sib(k, z).start()

    each(1, NY, forward_y)

    def forward_z(t):
        k = (y + t) % NY
        f_copy(k * 4 + (1 - z) * 2 + c, fz_ss.at[k], sib).wait_recv()
        f_to_sib(k, 1 - z).start()

    each(0, NY, forward_z)

    def wait_x(t):
        for k in range(ZH):
            g_copy(((x + t) % X) * ZH + k, gz_ss.at[0], sib).wait_recv()

    each(1, X, wait_x)

    def turn(k):
        gt[k] = gbuf[pl.ds(2 * k, 2)].reshape(2 * n, width).T

    each(0, C // 2, turn)
    gtv = jnp.concatenate([gt[k] for k in range(C // 2)], axis=1)

    def s1_copy(q):
        return rcopy(pall.at[q, :, 1 - c], s1_recv.at[q], s1_ss.at[q], s1_rs.at[q], sib)

    def product(t):
        q = (y + 1 + t) % NY
        pt = jnp.dot(gtv, a_dense[q], preferred_element_type=F32)
        pt_hi = pt.astype(BF)
        here = pl.ds(pl.multiple_of(q * 4 * n, 4 * n), 4 * n)
        ptb[0, :, here] = pt_hi
        ptb[1, :, here] = (pt - pt_hi.astype(F32)).astype(BF)
        pall[q] = pt_hi.T.reshape(2, 2, n, width)
        s1_copy(q).start()

    each(0, NY, product)

    def wait_sib(t):
        k = (y + t) % NY
        for zz in range(2):
            f_copy(k * 4 + zz * 2 + 1 - c, fz_ss.at[k], sib).wait_recv()

    each(0, NY, wait_sib)
    fall = fbuf[...].reshape(R * n, width)
    wt = jnp.dot(ptb[0], fall, preferred_element_type=F32) + jnp.dot(ptb[1], fall, preferred_element_type=F32)
    wpart[...] = wt.reshape(wpart.shape)
    a_copy = rcopy(wpart.at[1 - c], ra, a_ss, a_rs, sib)
    a_copy.start()

    def s2_copy(q):
        return rcopy(s2_send.at[q], s2_recv.at[q], s2_ss.at[q], s2_rs.at[q], zdev)

    def stage2(t):
        q = (y + 1 + t) % NY
        s1_copy(q).wait_recv()
        s2_send[q] = (pall[q, 1 - z, c].astype(F32) + s1_recv[q, 1 - z].astype(F32)).astype(BF)
        s2_copy(q).start()

    each(0, NY, stage2)

    a_copy.wait_recv()
    wb[...] = (wpart[c] + ra[...]).astype(BF)

    def b_copy(t):
        peer = (m + t) % M
        return rcopy(wb.at[peer], rb.at[m], b_ss.at[t], b_rs.at[m], (peer * 2 + c, col))

    each(1, M, lambda t: b_copy(t).start())
    rb[m] = wb[m]

    def total3(q):
        s2_copy(q).wait_recv()
        return pall[q, z, c].astype(F32) + s1_recv[q, z].astype(F32) + s2_recv[q].astype(F32)

    def s3_copy(q):
        return rcopy(s3_send.at[q], s3_recv.at[y], s3_ss.at[q], s3_rs.at[y], ydev(q))

    def stage3(t):
        q = (y + 1 + t) % NY
        s3_send[q] = total3(q).astype(BF)
        s3_copy(q).start()

    each(0, NY - 1, stage3)
    own[...] = total3(y)

    def b_wait(t):
        peer = (m + t) % M
        rcopy(wb.at[peer], rb.at[peer], b_ss.at[t], b_rs.at[peer], sib).wait_recv()

    each(1, M, b_wait)
    rc[col] = jnp.sum(rb[...].astype(F32), axis=0).astype(BF)

    def c_copy(t, slot):
        peer = (col + t) % C
        return rcopy(rc.at[slot], rc.at[slot], c_ss.at[t], c_rs.at[slot], (row, peer))

    each(1, C, lambda t: c_copy(t, col).start())

    def collect(t):
        q = (y + t) % NY
        rcopy(s3_send.at[q], s3_recv.at[q], s3_ss.at[q], s3_rs.at[q], sib).wait_recv()
        own[...] += s3_recv[q].astype(F32)

    each(1, NY, collect)

    loads[4].wait()
    pulled = own[...] * scale
    p_hi = pulled.astype(BF)
    p_lo = (pulled - p_hi.astype(F32)).astype(BF)
    over_last = (((1,), (1,)), ((), ()))
    w = w_v[...]
    gf_ref[...] = lax.dot_general(p_hi, w, over_last, preferred_element_type=F32) + lax.dot_general(
        p_lo, w, over_last, preferred_element_type=F32
    )

    each(1, C, lambda t: c_copy(t, (col + t) % C).wait_recv())
    wg_ref[c, m] = (jnp.sum(rc[...].astype(F32), axis=0) * norm).astype(BF)

    def d_copy(t, slot):
        peer = (m + t) % M
        return rcopy(wg_ref.at[c, slot], wg_ref.at[c, slot], d_ss.at[t], d_rs.at[slot], (peer * 2 + c, col))

    each(1, M, lambda t: d_copy(t, m).start())

    each(1, ZH, lambda t: to_z(t).wait_send())
    for k in range(ZH):
        each(1, X, lambda t: to_x(k, t).wait_send())
    each(1, NY, lambda t: f_to_y(t).wait_send())

    def drain(q):
        f_to_z(q).wait_send()
        f_to_sib(q, 0).wait_send()
        f_to_sib(q, 1).wait_send()
        s1_copy(q).wait_send()
        s2_copy(q).wait_send()

    each(0, NY, drain)
    each(1, NY, lambda t: s3_copy((y + t) % NY).wait_send())
    a_copy.wait_send()
    each(1, M, lambda t: b_copy(t).wait_send())
    each(1, C, lambda t: c_copy(t, col).wait_send())

    each(1, M, lambda t: d_copy(t, (m + t) % M).wait())
    rcopy(wg_ref.at[c], wg_ref.at[c], e_ss, e_rs, sib).start()
    rcopy(wg_ref.at[1 - c], wg_ref.at[1 - c], e_ss, e_rs, sib).wait()


def finish(gf_in, wg_in, gf_out, wg_out):
    gf_out[...] = gf_in[...]
    wg_out[...] = wg_in[...].reshape(wg_out.shape).astype(F32).T


def local(ZH, features, grad_out, relu_mask, degree, weight, adjacency, block_slot, block_count):
    R = lax.axis_size("row")
    C = lax.axis_size("col")
    n, width = features.shape
    entries, blk = adjacency.shape[2], adjacency.shape[3]
    NY, M, X = R // 4, R // 2, C // ZH
    part = (2, M, width // R, width)
    dma = pltpu.SemaphoreType.DMA
    vm = pltpu.VMEM
    vspec = pl.BlockSpec(memory_space=pltpu.VMEM)
    sspec = pl.BlockSpec(memory_space=pltpu.SMEM)
    aspec = pl.BlockSpec(memory_space=pl.ANY)
    gf, wg = pl.pallas_call(
        functools.partial(kernel, R, C, ZH, float((n * R * C) ** -0.5)),
        out_shape=(
            jax.ShapeDtypeStruct((n, width), F32),
            jax.ShapeDtypeStruct(part, BF),
        ),
        in_specs=[aspec] * 6 + [sspec, sspec],
        out_specs=(vspec, vspec),
        scratch_shapes=[
            vm((n, width), BF),
            vm((n, width), BF),
            vm((n, width), jnp.int32),
            vm((1, n), jnp.int32),
            vm((width, width), BF),
            vm((entries + 1, blk, blk), BF),
            vm((NY, C * n, 2 * blk), BF),
            vm((8, 128), jnp.int32),
            pltpu.SMEM((8, 128), jnp.int32),
            vm((C, n, width), BF),
            vm((R, n, width), BF),
            vm((C // 2, width, 2 * n), BF),
            vm((2, width, R * n), BF),
            vm((NY, 2, 2, n, width), BF),
            vm((NY, 2, n, width), BF),
            vm((NY, n, width), BF),
            vm((NY, n, width), BF),
            vm((NY, n, width), BF),
            vm((NY, n, width), BF),
            vm((n, width), F32),
            vm(part, F32),
            vm(part[1:], F32),
            vm(part[1:], BF),
            vm(part[1:], BF),
            vm((C,) + part[2:], BF),
            dma((5,)), dma, dma,
            dma((ZH,)), dma((ZH, X)), dma((C,)),
            dma((NY,)), dma((NY,)), dma((NY, 2)), dma((R,)),
            dma((NY,)), dma((NY,)),
            dma((NY,)), dma((NY,)),
            dma((NY,)), dma((NY,)),
            dma, dma,
            dma((M,)), dma((M,)),
            dma((C,)), dma((C,)),
            dma((M,)), dma((M,)),
            dma, dma,
        ],
        compiler_params=pltpu.CompilerParams(
            collective_id=0, has_side_effects=True, vmem_limit_bytes=56 * 1024 * 1024
        ),
    )(
        features, grad_out, relu_mask, degree.reshape(1, n), weight,
        adjacency.reshape(entries, blk, blk), block_slot.reshape(1, entries), block_count,
    )
    return pl.pallas_call(
        finish,
        out_shape=(
            jax.ShapeDtypeStruct((n, width), F32),
            jax.ShapeDtypeStruct((width, width), F32),
        ),
        in_specs=[vspec, vspec],
        out_specs=(vspec, vspec),
    )(gf, wg)


def solution(mesh):
    placed = (
        P(("row", "col"), None),
        P(("row", "col"), None),
        P(("row", "col"), None),
        P(("row", "col")),
        P(),
        P("row", "col", None, None, None),
        P("row", "col", None),
        P("row", "col"),
    )
    inner = min(4, mesh.shape["col"])
    return jax.shard_map(
        functools.partial(local, inner),
        mesh=mesh, in_specs=placed, out_specs=(P(("row", "col"), None), P()), check_vma=False,
    )
```

```python
import functools

import jax
import jax.numpy as jnp
from jax import lax
from jax.experimental import pallas as pl
from jax.experimental.pallas import tpu as pltpu
from jax.sharding import PartitionSpec as P

MESH = pl.DeviceIdType.MESH
BF = jnp.bfloat16
F32 = jnp.float32


def kernel(
    R, C, ZH, norm,
    feat_hbm, gout_hbm, mask_hbm, deg_hbm, w_hbm, adj_hbm, slot_ref, count_ref,
    gf_ref, wg_ref,
    feat_v, gout_v, mask_v, deg_v, w_v,
    adj_v, a_dense, inv_v, inv_s, gbuf, fbuf, gt, ptb, pall,
    s1_recv, s2_send, s2_recv, s3_send, s3_recv, own,
    wpart, ra, wb, rb, rc,
    in_sem, adj_sem, inv_sem, gz_ss, gx_ss, g_rs, fy_ss, fz_ss, fc_ss, f_rs,
    s1_ss, s1_rs, s2_ss, s2_rs, s3_ss, s3_rs,
    a_ss, a_rs, b_ss, b_rs, c_ss, c_rs, d_ss, d_rs, e_ss, e_rs,
):
    NY = R // 4
    M = R // 2
    X = C // ZH
    entries, blk = adj_hbm.shape[0], adj_hbm.shape[1]
    n, width = feat_hbm.shape
    row = lax.axis_index("row")
    col = lax.axis_index("col")
    y = row // 4
    z = (row // 2) % 2
    c = row % 2
    m = row // 2
    x = col // ZH
    zh = col % ZH
    sib = (m * 2 + (1 - c), col)
    zdev = (y * 4 + (1 - z) * 2 + c, col)

    def ydev(k):
        return (k * 4 + z * 2 + c, col)

    def rcopy(src, dst, ss, rs, dev):
        return pltpu.make_async_remote_copy(
            src_ref=src, dst_ref=dst, send_sem=ss, recv_sem=rs,
            device_id=dev, device_id_type=MESH,
        )

    def each(lo, hi, body, unroll=1):
        def step(t, u):
            body(t)
            return u

        lax.fori_loop(lo, hi, step, 0, unroll=unroll)

    def off(t, size):
        return size // 2 + (t // 2) * (2 * (t % 2) - 1)

    loads = [
        pltpu.make_async_copy(s, d, in_sem.at[k])
        for k, (s, d) in enumerate(
            [(gout_hbm, gout_v), (mask_hbm, mask_v), (deg_hbm, deg_v), (feat_hbm, feat_v), (w_hbm, w_v)]
        )
    ]
    for copy in loads:
        copy.start()
    adj_copy = pltpu.make_async_copy(adj_hbm, adj_v.at[pl.ds(0, entries)], adj_sem)
    adj_copy.start()

    bar = pltpu.get_barrier_semaphore()

    def greet(dev):
        pl.semaphore_signal(bar, inc=1, device_id=dev, device_id_type=MESH)

    each(1, ZH, lambda t: greet((row, x * ZH + (zh + off(t, ZH)) % ZH)))
    each(1, X, lambda t: greet((row, ((x + t) % X) * ZH + zh)))
    each(1, NY, lambda t: greet(ydev((y + t) % NY)))
    greet(zdev)
    greet(sib)

    for copy in loads[:3]:
        copy.wait()
    scale_row = lax.rsqrt(deg_v[...].astype(F32))
    eye = lax.broadcasted_iota(jnp.int32, (n, n), 0) == lax.broadcasted_iota(jnp.int32, (n, n), 1)
    scale = jnp.sum(jnp.where(eye, jnp.broadcast_to(scale_row, (n, n)), 0.0), axis=1, keepdims=True)
    masked = gout_v[...].astype(F32) * mask_v[...].astype(F32)
    gbuf[col] = (masked * scale).astype(BF)
    loads[3].wait()
    fbuf[row] = (feat_v[...].astype(F32) * scale).astype(BF)

    pl.semaphore_wait(bar, ZH - 1 + X - 1 + NY - 1 + 2)

    def g_copy(slot, ss, dev):
        return rcopy(gbuf.at[slot], gbuf.at[slot], ss, g_rs.at[slot], dev)

    def f_copy(slot, ss, dev):
        return rcopy(fbuf.at[slot], fbuf.at[slot], ss, f_rs.at[slot], dev)

    def to_z(t):
        return g_copy(col, gz_ss.at[t], (row, x * ZH + (zh + t) % ZH))

    def to_x(k, t):
        return g_copy(x * ZH + (zh + k) % ZH, gx_ss.at[k, t], (row, ((x + t) % X) * ZH + zh))

    def f_to_y(t):
        return f_copy(row, fy_ss.at[t], ydev((y + t) % NY))

    def f_to_z(k):
        return f_copy(k * 4 + z * 2 + c, fz_ss.at[k], zdev)

    def f_to_sib(k, zz):
        return f_copy(k * 4 + zz * 2 + c, fc_ss.at[k, zz], sib)

    each(1, ZH, lambda t: to_z(off(t, ZH)).start())
    each(1, NY, lambda t: f_to_y(off(t, NY)).start())
    each(1, X, lambda t: to_x(0, off(t, X)).start())
    f_to_z(y).start()
    f_to_sib(y, z).start()

    lane = lax.broadcasted_iota(jnp.int32, (8, 128), 1)
    live = count_ref[0, 0]

    def invert(b, acc):
        s = jnp.where(b < live, slot_ref[0, b], -1)
        return jnp.where(lane == s, b, acc)

    inv_v[...] = lax.fori_loop(0, entries, invert, jnp.full((8, 128), entries, jnp.int32))
    inv_copy = pltpu.make_async_copy(inv_v, inv_s, inv_sem)
    inv_copy.start()
    adj_v[entries] = jnp.zeros((blk, blk), BF)
    inv_copy.wait()
    adj_copy.wait()

    def fill(k):
        r = k // NY
        q = k % NY
        for h in range(2):
            e = inv_s[0, r * (2 * NY) + q * 2 + h]
            a_dense[q, pl.ds(pl.multiple_of(r * blk, blk), blk), pl.ds(h * blk, blk)] = adj_v[e]

    each(0, C * n // blk * NY, fill)

    def forward_x(k):
        slot = x * ZH + (zh + k) % ZH
        g_copy(slot, gz_ss.at[k], sib).wait_recv()
        each(1, X, lambda t: to_x(k, off(t, X)).start())

    def forward_y(t):
        k = (y + t) % NY
        f_copy(k * 4 + z * 2 + c, fz_ss.at[k], sib).wait_recv()
        f_to_z(k).start()
        f_to_sib(k, z).start()

    arrivals = [(2 * min(k, ZH - k), 0, k) for k in range(1, ZH)] + [(min(k, NY - k), 1, k) for k in range(1, NY)]
    for hops, kind, k in sorted(arrivals):
        if kind:
            forward_y(k)
        else:
            forward_x(k)

    def forward_z(t):
        k = (y + off(NY - t, NY)) % NY
        f_copy(k * 4 + (1 - z) * 2 + c, fz_ss.at[k], sib).wait_recv()
        f_to_sib(k, 1 - z).start()

    def wait_x(t):
        for k in range(ZH):
            g_copy(((x + t) % X) * ZH + k, gz_ss.at[0], sib).wait_recv()

    each(1, X, wait_x)

    def turn(k):
        gt[k] = gbuf[pl.ds(2 * k, 2)].reshape(2 * n, width).T

    each(0, C // 2, turn)
    gtv = jnp.concatenate([gt[k] for k in range(C // 2)], axis=1)

    def s1_copy(q):
        return rcopy(pall.at[q, :, 1 - c], s1_recv.at[q], s1_ss.at[q], s1_rs.at[q], sib)

    def product(t):
        forward_z(t)
        q = (y + off(t + 1, NY)) % NY
        pt = jnp.dot(gtv, a_dense[q], preferred_element_type=F32)
        pt_hi = pt.astype(BF)
        here = pl.ds(pl.multiple_of(q * 4 * n, 4 * n), 4 * n)
        ptb[0, :, here] = pt_hi
        ptb[1, :, here] = (pt - pt_hi.astype(F32)).astype(BF)
        pall[q] = pt_hi.T.reshape(2, 2, n, width)
        s1_copy(q).start()

    each(0, NY, product, 2)

    def wait_sib(t):
        k = (y + t) % NY
        for zz in range(2):
            f_copy(k * 4 + zz * 2 + 1 - c, fz_ss.at[k], sib).wait_recv()

    each(0, NY, wait_sib)
    fall = fbuf[...].reshape(R * n, width)
    wt = jnp.dot(ptb[0], fall, preferred_element_type=F32) + jnp.dot(ptb[1], fall, preferred_element_type=F32)
    wpart[...] = wt.reshape(wpart.shape)
    a_copy = rcopy(wpart.at[1 - c], ra, a_ss, a_rs, sib)
    a_copy.start()

    def s2_copy(q):
        return rcopy(s2_send.at[q], s2_recv.at[q], s2_ss.at[q], s2_rs.at[q], zdev)

    def stage2(t):
        q = (y + off(t + 1, NY)) % NY
        s1_copy(q).wait_recv()
        s2_send[q] = (pall[q, 1 - z, c].astype(F32) + s1_recv[q, 1 - z].astype(F32)).astype(BF)
        s2_copy(q).start()

    each(0, NY, stage2)

    a_copy.wait_recv()
    wb[...] = (wpart[c] + ra[...]).astype(BF)

    def row_peer(t):
        return ((y + off(t // 2 + 1, NY)) % NY) * 2 + (z + 1 - t % 2) % 2

    def b_copy(t):
        peer = row_peer(t)
        return rcopy(wb.at[peer], rb.at[m], b_ss.at[t], b_rs.at[m], (peer * 2 + c, col))

    each(0, M - 1, lambda t: b_copy(t).start())
    rb[m] = wb[m]

    def total3(q):
        s2_copy(q).wait_recv()
        return pall[q, z, c].astype(F32) + s1_recv[q, z].astype(F32) + s2_recv[q].astype(F32)

    def s3_copy(q):
        return rcopy(s3_send.at[q], s3_recv.at[y], s3_ss.at[q], s3_rs.at[y], ydev(q))

    def stage3(t):
        q = (y + off(t, NY)) % NY
        s3_send[q] = total3(q).astype(BF)
        s3_copy(q).start()

    each(1, NY // 2 + 1, stage3)

    def b_wait(t):
        peer = (m + t) % M
        rcopy(wb.at[peer], rb.at[peer], b_ss.at[t - 1], b_rs.at[peer], sib).wait_recv()

    each(1, M, b_wait)
    rc[col] = jnp.sum(rb[...].astype(F32), axis=0).astype(BF)

    def col_peer(t):
        return ((x + off(t % X + 1, X)) % X) * ZH + (zh + off(t // X + 1, ZH)) % ZH

    def c_copy(t, slot):
        return rcopy(rc.at[slot], rc.at[slot], c_ss.at[t], c_rs.at[slot], (row, col_peer(t)))

    each(0, C - 1, lambda t: c_copy(t, col).start())
    each(NY // 2 + 1, NY, stage3)
    own[...] = total3(y)

    def collect(t):
        q = (y + t) % NY
        rcopy(s3_send.at[q], s3_recv.at[q], s3_ss.at[q], s3_rs.at[q], sib).wait_recv()
        own[...] += s3_recv[q].astype(F32)

    each(1, NY, collect)

    loads[4].wait()
    pulled = own[...] * scale
    p_hi = pulled.astype(BF)
    p_lo = (pulled - p_hi.astype(F32)).astype(BF)
    over_last = (((1,), (1,)), ((), ()))
    w = w_v[...]
    gf_ref[...] = lax.dot_general(p_hi, w, over_last, preferred_element_type=F32) + lax.dot_general(
        p_lo, w, over_last, preferred_element_type=F32
    )

    each(0, C - 1, lambda t: c_copy(t, col_peer(t)).wait_recv())
    wg_ref[c, m] = (jnp.sum(rc[...].astype(F32), axis=0) * norm).astype(BF)

    def d_copy(t, slot):
        return rcopy(wg_ref.at[c, slot], wg_ref.at[c, slot], d_ss.at[t], d_rs.at[slot], (row_peer(t) * 2 + c, col))

    each(0, M - 1, lambda t: d_copy(t, m).start())

    each(1, ZH, lambda t: to_z(t).wait_send())
    for k in range(ZH):
        each(1, X, lambda t: to_x(k, t).wait_send())
    each(1, NY, lambda t: f_to_y(t).wait_send())

    def drain(q):
        f_to_z(q).wait_send()
        f_to_sib(q, 0).wait_send()
        f_to_sib(q, 1).wait_send()
        s1_copy(q).wait_send()
        s2_copy(q).wait_send()

    each(0, NY, drain)
    each(1, NY, lambda t: s3_copy((y + t) % NY).wait_send())
    a_copy.wait_send()
    each(0, M - 1, lambda t: b_copy(t).wait_send())
    each(0, C - 1, lambda t: c_copy(t, col).wait_send())

    each(0, M - 1, lambda t: d_copy(t, row_peer(t)).wait())
    rcopy(wg_ref.at[c], wg_ref.at[c], e_ss, e_rs, sib).start()
    rcopy(wg_ref.at[1 - c], wg_ref.at[1 - c], e_ss, e_rs, sib).wait()


def finish(gf_in, wg_in, gf_out, wg_out):
    gf_out[...] = gf_in[...]
    wg_out[...] = wg_in[...].reshape(wg_out.shape).astype(F32).T


def local(ZH, features, grad_out, relu_mask, degree, weight, adjacency, block_slot, block_count):
    R = lax.axis_size("row")
    C = lax.axis_size("col")
    n, width = features.shape
    entries, blk = adjacency.shape[2], adjacency.shape[3]
    NY, M, X = R // 4, R // 2, C // ZH
    part = (2, M, width // R, width)
    dma = pltpu.SemaphoreType.DMA
    vm = pltpu.VMEM
    vspec = pl.BlockSpec(memory_space=pltpu.VMEM)
    sspec = pl.BlockSpec(memory_space=pltpu.SMEM)
    aspec = pl.BlockSpec(memory_space=pl.ANY)
    gf, wg = pl.pallas_call(
        functools.partial(kernel, R, C, ZH, float((n * R * C) ** -0.5)),
        out_shape=(
            jax.ShapeDtypeStruct((n, width), F32),
            jax.ShapeDtypeStruct(part, BF),
        ),
        in_specs=[aspec] * 6 + [sspec, sspec],
        out_specs=(vspec, vspec),
        scratch_shapes=[
            vm((n, width), BF),
            vm((n, width), BF),
            vm((n, width), jnp.int32),
            vm((1, n), jnp.int32),
            vm((width, width), BF),
            vm((entries + 1, blk, blk), BF),
            vm((NY, C * n, 2 * blk), BF),
            vm((8, 128), jnp.int32),
            pltpu.SMEM((8, 128), jnp.int32),
            vm((C, n, width), BF),
            vm((R, n, width), BF),
            vm((C // 2, width, 2 * n), BF),
            vm((2, width, R * n), BF),
            vm((NY, 2, 2, n, width), BF),
            vm((NY, 2, n, width), BF),
            vm((NY, n, width), BF),
            vm((NY, n, width), BF),
            vm((NY, n, width), BF),
            vm((NY, n, width), BF),
            vm((n, width), F32),
            vm(part, F32),
            vm(part[1:], F32),
            vm(part[1:], BF),
            vm(part[1:], BF),
            vm((C,) + part[2:], BF),
            dma((5,)), dma, dma,
            dma((ZH,)), dma((ZH, X)), dma((C,)),
            dma((NY,)), dma((NY,)), dma((NY, 2)), dma((R,)),
            dma((NY,)), dma((NY,)),
            dma((NY,)), dma((NY,)),
            dma((NY,)), dma((NY,)),
            dma, dma,
            dma((M,)), dma((M,)),
            dma((C,)), dma((C,)),
            dma((M,)), dma((M,)),
            dma, dma,
        ],
        compiler_params=pltpu.CompilerParams(
            collective_id=0, has_side_effects=True, vmem_limit_bytes=56 * 1024 * 1024
        ),
    )(
        features, grad_out, relu_mask, degree.reshape(1, n), weight,
        adjacency.reshape(entries, blk, blk), block_slot.reshape(1, entries), block_count,
    )
    return pl.pallas_call(
        finish,
        out_shape=(
            jax.ShapeDtypeStruct((n, width), F32),
            jax.ShapeDtypeStruct((width, width), F32),
        ),
        in_specs=[vspec, vspec],
        out_specs=(vspec, vspec),
    )(gf, wg)


def solution(mesh):
    placed = (
        P(("row", "col"), None),
        P(("row", "col"), None),
        P(("row", "col"), None),
        P(("row", "col")),
        P(),
        P("row", "col", None, None, None),
        P("row", "col", None),
        P("row", "col"),
    )
    inner = min(4, mesh.shape["col"])
    return jax.shard_map(
        functools.partial(local, inner),
        mesh=mesh, in_specs=placed, out_specs=(P(("row", "col"), None), P()), check_vma=False,
    )
```

```python
import functools

import jax
import jax.numpy as jnp
from jax import lax
from jax.experimental import pallas as pl
from jax.experimental.pallas import tpu as pltpu
from jax.sharding import PartitionSpec as P

MESH = pl.DeviceIdType.MESH
BF = jnp.bfloat16
F32 = jnp.float32


def kernel(
    R, C, ZH, norm,
    feat_hbm, gout_hbm, mask_hbm, deg_hbm, w_hbm, adj_hbm, slot_ref, count_ref,
    gf_ref, wg_ref,
    feat_v, gout_v, mask_v, deg_v, w_v,
    adj_v, a_dense, inv_v, inv_s, gbuf, fbuf, gt, ft, pall,
    s1_recv, s_hi, s_lo, s2_recv, s3_send, s3_recv, own,
    wpart, ra, wb, rb, rc,
    in_sem, adj_sem, inv_sem, gz_ss, gx_ss, g_rs, fy_ss, fz_ss, f_rs,
    s1_ss, s1_rs, s2_ss, s2_rs, s3_ss, s3_rs,
    a_ss, a_rs, b_ss, b_rs, c_ss, c_rs, d_ss, d_rs, e_ss, e_rs,
):
    NY = R // 4
    M = R // 2
    X = C // ZH
    entries, blk = adj_hbm.shape[0], adj_hbm.shape[1]
    n, width = feat_hbm.shape
    row = lax.axis_index("row")
    col = lax.axis_index("col")
    y = row // 4
    z = (row // 2) % 2
    c = row % 2
    m = row // 2
    x = col // ZH
    zh = col % ZH
    sib = (m * 2 + (1 - c), col)
    zdev = (y * 4 + (1 - z) * 2 + c, col)

    def ydev(k):
        return (k * 4 + z * 2 + c, col)

    def rcopy(src, dst, ss, rs, dev):
        return pltpu.make_async_remote_copy(
            src_ref=src, dst_ref=dst, send_sem=ss, recv_sem=rs,
            device_id=dev, device_id_type=MESH,
        )

    def each(lo, hi, body, unroll=1):
        def step(t, u):
            body(t)
            return u

        lax.fori_loop(lo, hi, step, 0, unroll=unroll)

    def off(t, size):
        return size // 2 + (t // 2) * (2 * (t % 2) - 1)

    loads = [
        pltpu.make_async_copy(s, d, in_sem.at[k])
        for k, (s, d) in enumerate(
            [(gout_hbm, gout_v), (mask_hbm, mask_v), (deg_hbm, deg_v), (feat_hbm, feat_v), (w_hbm, w_v)]
        )
    ]
    for copy in loads:
        copy.start()
    adj_copy = pltpu.make_async_copy(adj_hbm, adj_v.at[pl.ds(0, entries)], adj_sem)
    adj_copy.start()

    bar = pltpu.get_barrier_semaphore()

    def greet(dev):
        pl.semaphore_signal(bar, inc=1, device_id=dev, device_id_type=MESH)

    each(1, ZH, lambda t: greet((row, x * ZH + (zh + off(t, ZH)) % ZH)))
    each(1, X, lambda t: greet((row, ((x + t) % X) * ZH + zh)))
    each(1, NY, lambda t: greet(ydev((y + t) % NY)))
    greet(zdev)
    greet(sib)

    for copy in loads[:3]:
        copy.wait()
    scale_row = lax.rsqrt(deg_v[...].astype(F32))
    eye = lax.broadcasted_iota(jnp.int32, (n, n), 0) == lax.broadcasted_iota(jnp.int32, (n, n), 1)
    scale = jnp.sum(jnp.where(eye, jnp.broadcast_to(scale_row, (n, n)), 0.0), axis=1, keepdims=True)
    masked = gout_v[...].astype(F32) * mask_v[...].astype(F32)
    gbuf[col] = (masked * scale).astype(BF)
    loads[3].wait()
    fbuf[m] = (feat_v[...].astype(F32) * scale).astype(BF)

    pl.semaphore_wait(bar, ZH - 1 + X - 1 + NY - 1 + 2)

    def g_copy(slot, ss, dev):
        return rcopy(gbuf.at[slot], gbuf.at[slot], ss, g_rs.at[slot], dev)

    def f_copy(slot, ss, dev):
        return rcopy(fbuf.at[slot], fbuf.at[slot], ss, f_rs.at[slot], dev)

    def to_z(t):
        return g_copy(col, gz_ss.at[t], (row, x * ZH + (zh + t) % ZH))

    def to_x(k, t):
        return g_copy(x * ZH + (zh + k) % ZH, gx_ss.at[k, t], (row, ((x + t) % X) * ZH + zh))

    def f_to_y(t):
        return f_copy(m, fy_ss.at[t], ydev((y + t) % NY))

    def f_to_z(k):
        return f_copy(k * 2 + z, fz_ss.at[k], zdev)

    each(1, ZH, lambda t: to_z(off(t, ZH)).start())
    each(1, NY, lambda t: f_to_y(off(t, NY)).start())
    each(1, X, lambda t: to_x(0, off(t, X)).start())
    f_to_z(y).start()

    lane = lax.broadcasted_iota(jnp.int32, (8, 128), 1)
    live = count_ref[0, 0]

    def invert(b, acc):
        s = jnp.where(b < live, slot_ref[0, b], -1)
        return jnp.where(lane == s, b, acc)

    inv_v[...] = lax.fori_loop(0, entries, invert, jnp.full((8, 128), entries, jnp.int32))
    inv_copy = pltpu.make_async_copy(inv_v, inv_s, inv_sem)
    inv_copy.start()
    adj_v[entries] = jnp.zeros((blk, blk), BF)
    inv_copy.wait()
    adj_copy.wait()

    def fill(k):
        r = k // NY
        q = k % NY
        for h in range(2):
            e = inv_s[0, r * (2 * NY) + q * 2 + h]
            a_dense[q, pl.ds(pl.multiple_of(r * blk, blk), blk), pl.ds(h * blk, blk)] = adj_v[e]

    each(0, C * n // blk * NY, fill)

    def forward_x(k):
        slot = x * ZH + (zh + k) % ZH
        g_copy(slot, gz_ss.at[k], sib).wait_recv()
        each(1, X, lambda t: to_x(k, off(t, X)).start())

    def forward_y(t):
        k = (y + t) % NY
        f_copy(k * 2 + z, fz_ss.at[k], sib).wait_recv()
        f_to_z(k).start()

    arrivals = [(2 * min(k, ZH - k), 0, k) for k in range(1, ZH)] + [(min(k, NY - k), 1, k) for k in range(1, NY)]
    each(1, ZH, lambda t: forward_x(off(ZH - t, ZH)))
    each(1, NY, lambda t: forward_y(off(NY - t, NY)))

    def wait_x(t):
        for k in range(ZH):
            g_copy(((x + t) % X) * ZH + k, gz_ss.at[0], sib).wait_recv()

    each(1, X, wait_x)

    def turn(k):
        gt[k] = gbuf[pl.ds(2 * k, 2)].reshape(2 * n, width).T

    each(0, C // 2, turn)
    gtv = jnp.concatenate([gt[k] for k in range(C // 2)], axis=1)

    def s1_copy(q):
        return rcopy(pall.at[q, :, 1 - c], s1_recv.at[q], s1_ss.at[q], s1_rs.at[q], sib)

    def product(t):
        q = (y + off(t + 1, NY)) % NY
        pt = jnp.dot(gtv, a_dense[q], preferred_element_type=F32).astype(BF)
        pall[q] = pt.T.reshape(2, 2, n, width)
        s1_copy(q).start()

    each(0, NY, product)

    each(0, NY, lambda k: f_copy(k * 2 + 1 - z, fz_ss.at[k], sib).wait_recv())

    def turn_f(k):
        ft[k] = fbuf[pl.ds(2 * k, 2)].reshape(2 * n, width).T

    each(0, NY, turn_f)

    def s2_copy(q):
        return rcopy(s_hi.at[q, 1 - z], s2_recv.at[q], s2_ss.at[q], s2_rs.at[q], zdev)

    def stage2(t):
        q = (y + off(t + 1, NY)) % NY
        s1_copy(q).wait_recv()
        both = pall[q, :, c].astype(F32) + s1_recv[q].astype(F32)
        hi = both.astype(BF)
        s_hi[q] = hi
        s_lo[q] = (both - hi.astype(F32)).astype(BF)
        s2_copy(q).start()

    each(0, NY, stage2)
    ftv = jnp.concatenate([ft[k] for k in range(NY)], axis=1)
    wt = jnp.dot(ftv, s_hi[...].reshape(M * n, width), preferred_element_type=F32)
    wt = wt + jnp.dot(ftv, s_lo[...].reshape(M * n, width), preferred_element_type=F32)
    wpart[...] = wt.reshape(wpart.shape)
    a_copy = rcopy(wpart.at[1 - c], ra, a_ss, a_rs, sib)
    a_copy.start()

    a_copy.wait_recv()
    wb[...] = (wpart[c] + ra[...]).astype(BF)

    def row_peer(t):
        return ((y + off(t // 2 + 1, NY)) % NY) * 2 + (z + 1 - t % 2) % 2

    def b_copy(t):
        peer = row_peer(t)
        return rcopy(wb.at[peer], rb.at[m], b_ss.at[t], b_rs.at[m], (peer * 2 + c, col))

    each(0, M - 1, lambda t: b_copy(t).start())
    rb[m] = wb[m]

    def total3(q):
        s2_copy(q).wait_recv()
        return pall[q, z, c].astype(F32) + s1_recv[q, z].astype(F32) + s2_recv[q].astype(F32)

    def s3_copy(q):
        return rcopy(s3_send.at[q], s3_recv.at[y], s3_ss.at[q], s3_rs.at[y], ydev(q))

    def stage3(t):
        q = (y + off(t, NY)) % NY
        s3_send[q] = total3(q).astype(BF)
        s3_copy(q).start()

    each(1, NY, stage3)
    own[...] = total3(y)

    def b_wait(t):
        peer = (m + t) % M
        rcopy(wb.at[peer], rb.at[peer], b_ss.at[t - 1], b_rs.at[peer], sib).wait_recv()

    each(1, M, b_wait)
    rc[col] = jnp.sum(rb[...].astype(F32), axis=0)

    def col_peer(t):
        return ((x + off(t % X + 1, X)) % X) * ZH + (zh + off(t // X + 1, ZH)) % ZH

    def c_copy(t, slot):
        return rcopy(rc.at[slot], rc.at[slot], c_ss.at[t], c_rs.at[slot], (row, col_peer(t)))

    each(0, C - 1, lambda t: c_copy(t, col).start())

    def collect(t):
        q = (y + t) % NY
        rcopy(s3_send.at[q], s3_recv.at[q], s3_ss.at[q], s3_rs.at[q], sib).wait_recv()
        own[...] += s3_recv[q].astype(F32)

    each(1, NY, collect)

    loads[4].wait()
    pulled = own[...] * scale
    p_hi = pulled.astype(BF)
    p_lo = (pulled - p_hi.astype(F32)).astype(BF)
    over_last = (((1,), (1,)), ((), ()))
    w = w_v[...]
    gf_ref[...] = lax.dot_general(p_hi, w, over_last, preferred_element_type=F32) + lax.dot_general(
        p_lo, w, over_last, preferred_element_type=F32
    )

    each(0, C - 1, lambda t: c_copy(t, col_peer(t)).wait_recv())
    wg_ref[c, m] = (jnp.sum(rc[...], axis=0) * norm).astype(BF)

    def d_copy(t, slot):
        return rcopy(wg_ref.at[c, slot], wg_ref.at[c, slot], d_ss.at[t], d_rs.at[slot], (row_peer(t) * 2 + c, col))

    each(0, M - 1, lambda t: d_copy(t, m).start())

    each(1, ZH, lambda t: to_z(t).wait_send())
    for k in range(ZH):
        each(1, X, lambda t: to_x(k, t).wait_send())
    each(1, NY, lambda t: f_to_y(t).wait_send())

    def drain(q):
        f_to_z(q).wait_send()
        s1_copy(q).wait_send()
        s2_copy(q).wait_send()

    each(0, NY, drain)
    each(1, NY, lambda t: s3_copy((y + t) % NY).wait_send())
    a_copy.wait_send()
    each(0, M - 1, lambda t: b_copy(t).wait_send())
    each(0, C - 1, lambda t: c_copy(t, col).wait_send())

    each(0, M - 1, lambda t: d_copy(t, row_peer(t)).wait())
    rcopy(wg_ref.at[c], wg_ref.at[c], e_ss, e_rs, sib).start()
    rcopy(wg_ref.at[1 - c], wg_ref.at[1 - c], e_ss, e_rs, sib).wait()


def finish(gf_in, wg_in, gf_out, wg_out):
    gf_out[...] = gf_in[...]
    wg_out[...] = wg_in[...].reshape(wg_out.shape).astype(F32)


def local(ZH, features, grad_out, relu_mask, degree, weight, adjacency, block_slot, block_count):
    R = lax.axis_size("row")
    C = lax.axis_size("col")
    n, width = features.shape
    entries, blk = adjacency.shape[2], adjacency.shape[3]
    NY, M, X = R // 4, R // 2, C // ZH
    part = (2, M, width // R, width)
    dma = pltpu.SemaphoreType.DMA
    vm = pltpu.VMEM
    vspec = pl.BlockSpec(memory_space=pltpu.VMEM)
    sspec = pl.BlockSpec(memory_space=pltpu.SMEM)
    aspec = pl.BlockSpec(memory_space=pl.ANY)
    gf, wg = pl.pallas_call(
        functools.partial(kernel, R, C, ZH, float((n * R * C) ** -0.5)),
        out_shape=(
            jax.ShapeDtypeStruct((n, width), F32),
            jax.ShapeDtypeStruct(part, BF),
        ),
        in_specs=[aspec] * 6 + [sspec, sspec],
        out_specs=(vspec, vspec),
        scratch_shapes=[
            vm((n, width), BF),
            vm((n, width), BF),
            vm((n, width), jnp.int32),
            vm((1, n), jnp.int32),
            vm((width, width), BF),
            vm((entries + 1, blk, blk), BF),
            vm((NY, C * n, 2 * blk), BF),
            vm((8, 128), jnp.int32),
            pltpu.SMEM((8, 128), jnp.int32),
            vm((C, n, width), BF),
            vm((M, n, width), BF),
            vm((C // 2, width, 2 * n), BF),
            vm((NY, width, 2 * n), BF),
            vm((NY, 2, 2, n, width), BF),
            vm((NY, 2, n, width), BF),
            vm((NY, 2, n, width), BF),
            vm((NY, 2, n, width), BF),
            vm((NY, n, width), BF),
            vm((NY, n, width), BF),
            vm((NY, n, width), BF),
            vm((n, width), F32),
            vm(part, F32),
            vm(part[1:], F32),
            vm(part[1:], BF),
            vm(part[1:], BF),
            vm((C,) + part[2:], F32),
            dma((5,)), dma, dma,
            dma((ZH,)), dma((ZH, X)), dma((C,)),
            dma((NY,)), dma((NY,)), dma((M,)),
            dma((NY,)), dma((NY,)),
            dma((NY,)), dma((NY,)),
            dma((NY,)), dma((NY,)),
            dma, dma,
            dma((M,)), dma((M,)),
            dma((C,)), dma((C,)),
            dma((M,)), dma((M,)),
            dma, dma,
        ],
        compiler_params=pltpu.CompilerParams(
            collective_id=0, has_side_effects=True, vmem_limit_bytes=56 * 1024 * 1024
        ),
    )(
        features, grad_out, relu_mask, degree.reshape(1, n), weight,
        adjacency.reshape(entries, blk, blk), block_slot.reshape(1, entries), block_count,
    )
    return pl.pallas_call(
        finish,
        out_shape=(
            jax.ShapeDtypeStruct((n, width), F32),
            jax.ShapeDtypeStruct((width, width), F32),
        ),
        in_specs=[vspec, vspec],
        out_specs=(vspec, vspec),
    )(gf, wg)


def solution(mesh):
    placed = (
        P(("row", "col"), None),
        P(("row", "col"), None),
        P(("row", "col"), None),
        P(("row", "col")),
        P(),
        P("row", "col", None, None, None),
        P("row", "col", None),
        P("row", "col"),
    )
    inner = min(4, mesh.shape["col"])
    return jax.shard_map(
        functools.partial(local, inner),
        mesh=mesh, in_specs=placed, out_specs=(P(("row", "col"), None), P()), check_vma=False,
    )
```

```python
import functools

import jax
import jax.numpy as jnp
from jax import lax
from jax.experimental import pallas as pl
from jax.experimental.pallas import tpu as pltpu
from jax.sharding import PartitionSpec as P

MESH = pl.DeviceIdType.MESH
BF = jnp.bfloat16
F32 = jnp.float32
rem = lax.rem
div = lax.div


def kernel(
    R, C, ZH, norm,
    feat_hbm, gout_hbm, mask_hbm, deg_hbm, w_hbm, adj_hbm, slot_hbm, count_hbm,
    gf_ref, wg_ref,
    feat_v, gout_v, mask_v, deg_v, w_v, slot_ref, count_ref,
    adj_v, a_dense, inv_v, inv_s, gbuf, fbuf, gt, ft, pall,
    s1_recv, s_hi, s_lo, s2_recv, s3_send, s3_recv, own,
    wpart, ra, wb, rb, rc,
    in_sem, adj_sem, inv_sem, gz_ss, gx_ss, g_rs, fy_ss, fz_ss, f_rs,
    s1_ss, s1_rs, s2_ss, s2_rs, s3_ss, s3_rs,
    a_ss, a_rs, b_ss, b_rs, c_ss, c_rs, d_ss, d_rs,
):
    NY = R // 4
    M = R // 2
    X = C // ZH
    entries, blk = adj_hbm.shape[0], adj_hbm.shape[1]
    n, width = feat_hbm.shape
    row = lax.axis_index("row")
    col = lax.axis_index("col")
    y = div(row, 4)
    z = rem(div(row, 2), 2)
    c = rem(row, 2)
    m = div(row, 2)
    x = div(col, ZH)
    zh = rem(col, ZH)
    sib = (m * 2 + (1 - c), col)
    zdev = (y * 4 + (1 - z) * 2 + c, col)

    def ydev(k):
        return (k * 4 + z * 2 + c, col)

    def rcopy(src, dst, ss, rs, dev):
        return pltpu.make_async_remote_copy(
            src_ref=src, dst_ref=dst, send_sem=ss, recv_sem=rs,
            device_id=dev, device_id_type=MESH,
        )

    def each(lo, hi, body, unroll=1):
        def step(t, u):
            body(t)
            return u

        lax.fori_loop(lo, hi, step, 0, unroll=unroll)

    def off(t, size):
        return size // 2 + div(t, 2) * (2 * rem(t, 2) - 1)

    bar = pltpu.get_barrier_semaphore()

    def greet(dev):
        pl.semaphore_signal(bar, inc=1, device_id=dev, device_id_type=MESH)

    each(1, ZH, lambda t: greet((row, x * ZH + rem(zh + off(t, ZH), ZH))))
    each(1, NY, lambda t: greet(ydev(rem(y + off(t, NY), NY))))
    each(1, X, lambda t: greet((row, rem(x + off(t, X), X) * ZH + zh)))
    greet(zdev)
    greet(sib)

    loads = [
        pltpu.make_async_copy(s, d, in_sem.at[k])
        for k, (s, d) in enumerate(
            [(gout_hbm, gout_v), (mask_hbm, mask_v), (deg_hbm, deg_v), (feat_hbm, feat_v), (w_hbm, w_v),
             (slot_hbm, slot_ref), (count_hbm, count_ref)]
        )
    ]
    for copy in loads:
        copy.start()
    adj_copy = pltpu.make_async_copy(adj_hbm, adj_v.at[pl.ds(0, entries)], adj_sem)
    adj_copy.start()

    for copy in loads[:3]:
        copy.wait()
    scale_row = lax.rsqrt(deg_v[...].astype(F32))
    eye = lax.broadcasted_iota(jnp.int32, (n, n), 0) == lax.broadcasted_iota(jnp.int32, (n, n), 1)
    scale = jnp.sum(jnp.where(eye, jnp.broadcast_to(scale_row, (n, n)), 0.0), axis=1, keepdims=True)
    masked = gout_v[...].astype(F32) * mask_v[...].astype(F32)
    gbuf[col] = (masked * scale).astype(BF)
    loads[3].wait()
    fbuf[m] = (feat_v[...].astype(F32) * scale).astype(BF)

    pl.semaphore_wait(bar, ZH - 1 + X - 1 + NY - 1 + 2)

    def g_copy(slot, ss, dev):
        return rcopy(gbuf.at[slot], gbuf.at[slot], ss, g_rs.at[slot], dev)

    def f_copy(slot, ss, dev):
        return rcopy(fbuf.at[slot], fbuf.at[slot], ss, f_rs.at[slot], dev)

    def to_z(t):
        return g_copy(col, gz_ss.at[t], (row, x * ZH + rem(zh + t, ZH)))

    def to_x(k, t):
        return g_copy(x * ZH + rem(zh + k, ZH), gx_ss.at[k, t], (row, rem(x + t, X) * ZH + zh))

    def f_to_y(t):
        return f_copy(m, fy_ss.at[t], ydev(rem(y + t, NY)))

    def f_to_z(k):
        return f_copy(k * 2 + z, fz_ss.at[k], zdev)

    each(1, ZH, lambda t: to_z(off(t, ZH)).start())
    each(1, NY, lambda t: f_to_y(off(t, NY)).start())
    each(1, X, lambda t: to_x(0, off(t, X)).start())
    f_to_z(y).start()

    loads[5].wait()
    loads[6].wait()
    lane = lax.broadcasted_iota(jnp.int32, (8, 128), 1)
    live = count_ref[0, 0]

    def invert(b, acc):
        s = jnp.where(b < live, slot_ref[0, b], -1)
        return jnp.where(lane == s, b, acc)

    inv_v[...] = lax.fori_loop(0, entries, invert, jnp.full((8, 128), entries, jnp.int32))
    inv_copy = pltpu.make_async_copy(inv_v, inv_s, inv_sem)
    inv_copy.start()
    adj_v[entries] = jnp.zeros((blk, blk), BF)
    inv_copy.wait()
    adj_copy.wait()

    def fill(k):
        r = div(k, NY)
        q = rem(k, NY)
        for h in range(2):
            e = inv_s[0, r * (2 * NY) + q * 2 + h]
            a_dense[q, pl.ds(pl.multiple_of(r * blk, blk), blk), pl.ds(h * blk, blk)] = adj_v[e]

    each(0, C * n // blk * NY, fill)

    def forward_x(k):
        slot = x * ZH + rem(zh + k, ZH)
        g_copy(slot, gz_ss.at[k], sib).wait_recv()
        each(1, X, lambda t: to_x(k, off(t, X)).start())

    def forward_y(t):
        k = rem(y + t, NY)
        f_copy(k * 2 + z, fz_ss.at[k], sib).wait_recv()
        f_to_z(k).start()

    arrivals = [(2 * min(k, ZH - k), 0, k) for k in range(1, ZH)] + [(min(k, NY - k), 1, k) for k in range(1, NY)]
    each(1, ZH, lambda t: forward_x(off(ZH - t, ZH)))
    each(1, NY, lambda t: forward_y(off(NY - t, NY)))

    def wait_x(t):
        for k in range(ZH):
            g_copy(rem(x + t, X) * ZH + k, gz_ss.at[0], sib).wait_recv()

    each(1, X, wait_x)

    def turn(k):
        gt[k] = gbuf[pl.ds(2 * k, 2)].reshape(2 * n, width).T

    each(0, C // 2, turn)
    gtv = jnp.concatenate([gt[k] for k in range(C // 2)], axis=1)

    def s1_copy(q):
        return rcopy(pall.at[q, :, 1 - c], s1_recv.at[q], s1_ss.at[q], s1_rs.at[q], sib)

    def product(t):
        q = rem(y + off(t + 1, NY), NY)
        pt = jnp.dot(gtv, a_dense[q], preferred_element_type=F32).astype(BF)
        pall[q] = pt.T.reshape(2, 2, n, width)
        s1_copy(q).start()

    each(0, NY, product)

    each(0, NY, lambda k: f_copy(k * 2 + 1 - z, fz_ss.at[k], sib).wait_recv())

    def turn_f(k):
        ft[k] = fbuf[pl.ds(2 * k, 2)].reshape(2 * n, width).T

    each(0, NY, turn_f)

    def s2_copy(q):
        return rcopy(s_hi.at[q, 1 - z], s2_recv.at[q], s2_ss.at[q], s2_rs.at[q], zdev)

    def stage2(t):
        q = rem(y + off(t + 1, NY), NY)
        s1_copy(q).wait_recv()
        both = pall[q, :, c].astype(F32) + s1_recv[q].astype(F32)
        hi = both.astype(BF)
        s_hi[q] = hi
        s_lo[q] = (both - hi.astype(F32)).astype(BF)
        s2_copy(q).start()

    each(0, NY, stage2)
    ftv = jnp.concatenate([ft[k] for k in range(NY)], axis=1)
    wt = jnp.dot(ftv, s_hi[...].reshape(M * n, width), preferred_element_type=F32)
    wt = wt + jnp.dot(ftv, s_lo[...].reshape(M * n, width), preferred_element_type=F32)
    wpart[...] = wt.reshape(wpart.shape)
    a_copy = rcopy(wpart.at[1 - c], ra, a_ss, a_rs, sib)
    a_copy.start()

    a_copy.wait_recv()
    wb[...] = (wpart[c] + ra[...]).astype(BF)

    def row_peer(t):
        return (rem(y + off(div(t, 2) + 1, NY), NY)) * 2 + rem(z + 1 - rem(t, 2), 2)

    def b_copy(t):
        peer = row_peer(t)
        return rcopy(wb.at[peer], rb.at[m], b_ss.at[t], b_rs.at[m], (peer * 2 + c, col))

    each(0, M - 1, lambda t: b_copy(t).start())
    rb[m] = wb[m]

    def total3(q):
        s2_copy(q).wait_recv()
        return pall[q, z, c].astype(F32) + s1_recv[q, z].astype(F32) + s2_recv[q].astype(F32)

    def s3_copy(q):
        return rcopy(s3_send.at[q], s3_recv.at[y], s3_ss.at[q], s3_rs.at[y], ydev(q))

    def stage3(t):
        q = rem(y + off(t, NY), NY)
        s3_send[q] = total3(q).astype(BF)
        s3_copy(q).start()

    each(1, NY, stage3)
    own[...] = total3(y)

    def b_wait(t):
        peer = rem(m + t, M)
        rcopy(wb.at[peer], rb.at[peer], b_ss.at[t - 1], b_rs.at[peer], sib).wait_recv()

    each(1, M, b_wait)
    rc[col] = jnp.sum(rb[...].astype(F32), axis=0)

    def col_peer(t):
        return ((x + off(rem(t, X) + 1, X)) % X) * ZH + rem(zh + off(div(t, X) + 1, ZH), ZH)

    def c_copy(t, slot):
        return rcopy(rc.at[slot], rc.at[slot], c_ss.at[t], c_rs.at[slot], (row, col_peer(t)))

    each(0, C - 1, lambda t: c_copy(t, col).start())

    def collect(t):
        q = rem(y + t, NY)
        rcopy(s3_send.at[q], s3_recv.at[q], s3_ss.at[q], s3_rs.at[q], sib).wait_recv()
        own[...] += s3_recv[q].astype(F32)

    each(1, NY, collect)

    loads[4].wait()
    pulled = own[...] * scale
    p_hi = pulled.astype(BF)
    p_lo = (pulled - p_hi.astype(F32)).astype(BF)
    over_last = (((1,), (1,)), ((), ()))
    w = w_v[...]
    gf_ref[...] = lax.dot_general(p_hi, w, over_last, preferred_element_type=F32) + lax.dot_general(
        p_lo, w, over_last, preferred_element_type=F32
    )

    each(0, C - 1, lambda t: c_copy(t, col_peer(t)).wait_recv())
    wg_ref[c, m] = (jnp.sum(rc[...], axis=0) * norm).astype(BF)

    def d_copy(t, slot, core):
        return rcopy(wg_ref.at[c, slot], wg_ref.at[c, slot], d_ss.at[core, t], d_rs.at[c, slot], (row_peer(t) * 2 + core, col))

    def d_start(t):
        d_copy(t, m, 1 - c).start()

        @pl.when(t < M - 1)
        def _():
            d_copy(t, m, c).start()

    each(0, M, d_start)

    each(1, ZH, lambda t: to_z(t).wait_send())
    for k in range(ZH):
        each(1, X, lambda t: to_x(k, t).wait_send())
    each(1, NY, lambda t: f_to_y(t).wait_send())

    def drain(q):
        f_to_z(q).wait_send()
        s1_copy(q).wait_send()
        s2_copy(q).wait_send()

    each(0, NY, drain)
    each(1, NY, lambda t: s3_copy(rem(y + t, NY)).wait_send())
    a_copy.wait_send()
    each(0, M - 1, lambda t: b_copy(t).wait_send())
    each(0, C - 1, lambda t: c_copy(t, col).wait_send())

    def d_wait(t):
        d_copy(t, m, 1 - c).wait_send()
        rcopy(wg_ref.at[1 - c, t], wg_ref.at[1 - c, t], d_ss.at[0, t], d_rs.at[1 - c, t], sib).wait_recv()

        @pl.when(t < M - 1)
        def _():
            d_copy(t, m, c).wait_send()
            d_copy(t, row_peer(t), c).wait_recv()

    each(0, M, d_wait)


def finish(gf_in, wg_in, gf_out, wg_out):
    gf_out[...] = gf_in[...]
    wg_out[...] = wg_in[...].reshape(wg_out.shape).astype(F32)


def local(ZH, features, grad_out, relu_mask, degree, weight, adjacency, block_slot, block_count):
    R = lax.axis_size("row")
    C = lax.axis_size("col")
    n, width = features.shape
    entries, blk = adjacency.shape[2], adjacency.shape[3]
    NY, M, X = R // 4, R // 2, C // ZH
    part = (2, M, width // R, width)
    dma = pltpu.SemaphoreType.DMA
    vm = pltpu.VMEM
    vspec = pl.BlockSpec(memory_space=pltpu.VMEM)
    aspec = pl.BlockSpec(memory_space=pltpu.HBM)
    gf, wg = pl.pallas_call(
        functools.partial(kernel, R, C, ZH, float((n * R * C) ** -0.5)),
        out_shape=(
            jax.ShapeDtypeStruct((n, width), F32),
            jax.ShapeDtypeStruct(part, BF),
        ),
        in_specs=[aspec] * 8,
        out_specs=(vspec, vspec),
        scratch_shapes=[
            vm((n, width), BF),
            vm((n, width), BF),
            vm((n, width), jnp.int32),
            vm((1, n), jnp.int32),
            vm((width, width), BF),
            pltpu.SMEM((1, entries), jnp.int32),
            pltpu.SMEM((1, 1), jnp.int32),
            vm((entries + 1, blk, blk), BF),
            vm((NY, C * n, 2 * blk), BF),
            vm((8, 128), jnp.int32),
            pltpu.SMEM((8, 128), jnp.int32),
            vm((C, n, width), BF),
            vm((M, n, width), BF),
            vm((C // 2, width, 2 * n), BF),
            vm((NY, width, 2 * n), BF),
            vm((NY, 2, 2, n, width), BF),
            vm((NY, 2, n, width), BF),
            vm((NY, 2, n, width), BF),
            vm((NY, 2, n, width), BF),
            vm((NY, n, width), BF),
            vm((NY, n, width), BF),
            vm((NY, n, width), BF),
            vm((n, width), F32),
            vm(part, F32),
            vm(part[1:], F32),
            vm(part[1:], BF),
            vm(part[1:], BF),
            vm((C,) + part[2:], F32),
            dma((7,)), dma, dma,
            dma((ZH,)), dma((ZH, X)), dma((C,)),
            dma((NY,)), dma((NY,)), dma((M,)),
            dma((NY,)), dma((NY,)),
            dma((NY,)), dma((NY,)),
            dma((NY,)), dma((NY,)),
            dma, dma,
            dma((M,)), dma((M,)),
            dma((C,)), dma((C,)),
            dma((2, M)), dma((2, M)),
        ],
        compiler_params=pltpu.CompilerParams(
            collective_id=0, has_side_effects=True, vmem_limit_bytes=56 * 1024 * 1024
        ),
    )(
        features, grad_out, relu_mask, degree.reshape(1, n), weight,
        adjacency.reshape(entries, blk, blk), block_slot.reshape(1, entries), block_count,
    )
    return pl.pallas_call(
        finish,
        out_shape=(
            jax.ShapeDtypeStruct((n, width), F32),
            jax.ShapeDtypeStruct((width, width), F32),
        ),
        in_specs=[vspec, vspec],
        out_specs=(vspec, vspec),
    )(gf, wg)


def solution(mesh):
    placed = (
        P(("row", "col"), None),
        P(("row", "col"), None),
        P(("row", "col"), None),
        P(("row", "col")),
        P(),
        P("row", "col", None, None, None),
        P("row", "col", None),
        P("row", "col"),
    )
    inner = min(4, mesh.shape["col"])
    return jax.shard_map(
        functools.partial(local, inner),
        mesh=mesh, in_specs=placed, out_specs=(P(("row", "col"), None), P()), check_vma=False,
    )
```

```python
import functools

import jax
import jax.numpy as jnp
from jax import lax
from jax.experimental import pallas as pl
from jax.experimental.pallas import tpu as pltpu
from jax.sharding import PartitionSpec as P

MESH = pl.DeviceIdType.MESH
BF = jnp.bfloat16
F32 = jnp.float32
rem = lax.rem
div = lax.div


def kernel(
    R, C, ZH, norm,
    feat_hbm, gout_hbm, mask_hbm, deg_hbm, w_hbm, adj_hbm, slot_hbm, count_hbm,
    gf_ref, wg_ref,
    feat_v, gout_v, mask_v, deg_v, w_v, slot_ref, count_ref,
    adj_v, a_dense, inv_v, inv_s, gbuf, fbuf, gt, ft, pall,
    s1_recv, s_hi, s_lo, s2_recv, s3_send, s3_recv, own,
    wpart, ra, wb, rb, rc,
    in_sem, adj_sem, inv_sem, gz_ss, gx_ss, g_rs, fy_ss, fz_ss, f_rs,
    s1_ss, s1_rs, s2_ss, s2_rs, s3_ss, s3_rs,
    a_ss, a_rs, b_ss, b_rs, c_ss, c_rs, d_ss, d_rs,
):
    NY = R // 4
    M = R // 2
    X = C // ZH
    entries, blk = adj_hbm.shape[0], adj_hbm.shape[1]
    n, width = feat_hbm.shape
    row = lax.axis_index("row")
    col = lax.axis_index("col")
    y = div(row, 4)
    z = rem(div(row, 2), 2)
    c = rem(row, 2)
    m = div(row, 2)
    x = div(col, ZH)
    zh = rem(col, ZH)
    sib = (m * 2 + (1 - c), col)
    zdev = (y * 4 + (1 - z) * 2 + c, col)

    def ydev(k):
        return (k * 4 + z * 2 + c, col)

    def rcopy(src, dst, ss, rs, dev):
        return pltpu.make_async_remote_copy(
            src_ref=src, dst_ref=dst, send_sem=ss, recv_sem=rs,
            device_id=dev, device_id_type=MESH,
        )

    def each(lo, hi, body, unroll=1):
        def step(t, u):
            body(t)
            return u

        lax.fori_loop(lo, hi, step, 0, unroll=unroll)

    def off(t, size):
        return size // 2 + div(t, 2) * (2 * rem(t, 2) - 1)

    bar = pltpu.get_barrier_semaphore()

    def greet(dev):
        pl.semaphore_signal(bar, inc=1, device_id=dev, device_id_type=MESH)

    each(1, ZH, lambda t: greet((row, x * ZH + rem(zh + off(t, ZH), ZH))))
    each(1, NY, lambda t: greet(ydev(rem(y + off(t, NY), NY))))
    each(1, X, lambda t: greet((row, rem(x + off(t, X), X) * ZH + zh)))
    greet(zdev)
    greet(sib)

    loads = [
        pltpu.make_async_copy(s, d, in_sem.at[k])
        for k, (s, d) in enumerate(
            [(gout_hbm, gout_v), (mask_hbm, mask_v), (deg_hbm, deg_v), (feat_hbm, feat_v), (w_hbm, w_v),
             (slot_hbm, slot_ref), (count_hbm, count_ref)]
        )
    ]
    for copy in loads:
        copy.start()
    adj_copy = pltpu.make_async_copy(adj_hbm, adj_v.at[pl.ds(0, entries)], adj_sem)
    adj_copy.start()

    for copy in loads[:3]:
        copy.wait()
    scale_row = lax.rsqrt(deg_v[...].astype(F32))
    eye = lax.broadcasted_iota(jnp.int32, (n, n), 0) == lax.broadcasted_iota(jnp.int32, (n, n), 1)
    scale = jnp.sum(jnp.where(eye, jnp.broadcast_to(scale_row, (n, n)), 0.0), axis=1, keepdims=True)
    masked = gout_v[...].astype(F32) * mask_v[...].astype(F32)
    gbuf[col] = (masked * scale).astype(BF)
    loads[3].wait()
    fbuf[m] = (feat_v[...].astype(F32) * scale).astype(BF)

    pl.semaphore_wait(bar, ZH - 1 + X - 1 + NY - 1 + 2)

    def g_copy(slot, ss, dev):
        return rcopy(gbuf.at[slot], gbuf.at[slot], ss, g_rs.at[slot], dev)

    def f_copy(slot, ss, dev):
        return rcopy(fbuf.at[slot], fbuf.at[slot], ss, f_rs.at[slot], dev)

    def to_z(t):
        return g_copy(col, gz_ss.at[t], (row, x * ZH + rem(zh + t, ZH)))

    def to_x(k, t):
        return g_copy(x * ZH + rem(zh + k, ZH), gx_ss.at[k, t], (row, rem(x + t, X) * ZH + zh))

    def f_to_y(t):
        return f_copy(m, fy_ss.at[t], ydev(rem(y + t, NY)))

    def f_to_z(k):
        return f_copy(k * 2 + z, fz_ss.at[k], zdev)

    each(1, ZH, lambda t: to_z(off(t, ZH)).start())
    each(1, NY, lambda t: f_to_y(off(t, NY)).start())
    each(1, X, lambda t: to_x(0, off(t, X)).start())
    f_to_z(y).start()

    loads[5].wait()
    loads[6].wait()
    lane = lax.broadcasted_iota(jnp.int32, (8, 128), 1)
    live = count_ref[0, 0]

    def invert(b, acc):
        s = jnp.where(b < live, slot_ref[0, b], -1)
        return jnp.where(lane == s, b, acc)

    inv_v[...] = lax.fori_loop(0, entries, invert, jnp.full((8, 128), entries, jnp.int32))
    inv_copy = pltpu.make_async_copy(inv_v, inv_s, inv_sem)
    inv_copy.start()
    adj_v[entries] = jnp.zeros((blk, blk), BF)
    inv_copy.wait()
    adj_copy.wait()

    def fill(k):
        r = div(k, NY)
        q = rem(k, NY)
        for h in range(2):
            e = inv_s[0, r * (2 * NY) + q * 2 + h]
            a_dense[q, pl.ds(pl.multiple_of(r * blk, blk), blk), pl.ds(h * blk, blk)] = adj_v[e]

    each(0, C * n // blk * NY, fill)

    def forward_x(k):
        slot = x * ZH + rem(zh + k, ZH)
        g_copy(slot, gz_ss.at[k], sib).wait_recv()
        each(1, X, lambda t: to_x(k, off(t, X)).start())

    def forward_y(t):
        k = rem(y + t, NY)
        f_copy(k * 2 + z, fz_ss.at[k], sib).wait_recv()
        f_to_z(k).start()

    arrivals = [(2 * min(k, ZH - k), 0, k) for k in range(1, ZH)] + [(min(k, NY - k), 1, k) for k in range(1, NY)]
    each(1, ZH, lambda t: forward_x(off(ZH - t, ZH)))
    each(1, NY, lambda t: forward_y(off(NY - t, NY)))

    def wait_x(t):
        there = rem(x + t, X)

        @pl.when(t > 0)
        def _():
            for k in range(ZH):
                g_copy(there * ZH + k, gz_ss.at[0], sib).wait_recv()

        for k in range(ZH // 2):
            pair = there * (ZH // 2) + k
            gt[pair] = gbuf[pl.ds(2 * pair, 2)].reshape(2 * n, width).T

    each(0, X, wait_x)
    gtv = jnp.concatenate([gt[k] for k in range(C // 2)], axis=1)

    def s1_copy(q):
        return rcopy(pall.at[q, :, 1 - c], s1_recv.at[q], s1_ss.at[q], s1_rs.at[q], sib)

    def product(t):
        q = rem(y + off(t + 1, NY), NY)
        pt = jnp.dot(gtv, a_dense[q], preferred_element_type=F32).astype(BF)
        pall[q] = pt.T.reshape(2, 2, n, width)
        s1_copy(q).start()

    each(0, NY, product)

    each(0, NY, lambda k: f_copy(k * 2 + 1 - z, fz_ss.at[k], sib).wait_recv())

    def turn_f(k):
        ft[k] = fbuf[pl.ds(2 * k, 2)].reshape(2 * n, width).T

    each(0, NY, turn_f)

    def s2_copy(q):
        return rcopy(s_hi.at[q, 1 - z], s2_recv.at[q], s2_ss.at[q], s2_rs.at[q], zdev)

    def stage2(t):
        q = rem(y + off(t + 1, NY), NY)
        s1_copy(q).wait_recv()
        both = pall[q, :, c].astype(F32) + s1_recv[q].astype(F32)
        hi = both.astype(BF)
        s_hi[q] = hi
        s_lo[q] = (both - hi.astype(F32)).astype(BF)
        s2_copy(q).start()

    each(0, NY, stage2)
    ftv = jnp.concatenate([ft[k] for k in range(NY)], axis=1)
    wt = jnp.dot(ftv, s_hi[...].reshape(M * n, width), preferred_element_type=F32)
    wt = wt + jnp.dot(ftv, s_lo[...].reshape(M * n, width), preferred_element_type=F32)
    wpart[...] = wt.reshape(wpart.shape)
    a_copy = rcopy(wpart.at[1 - c], ra, a_ss, a_rs, sib)
    a_copy.start()

    a_copy.wait_recv()
    wb[...] = (wpart[c] + ra[...]).astype(BF)

    def row_peer(t):
        return (rem(y + off(div(t, 2) + 1, NY), NY)) * 2 + rem(z + 1 - rem(t, 2), 2)

    def b_copy(t):
        peer = row_peer(t)
        return rcopy(wb.at[peer], rb.at[m], b_ss.at[t], b_rs.at[m], (peer * 2 + c, col))

    each(0, M - 1, lambda t: b_copy(t).start())
    rb[m] = wb[m]

    def total3(q):
        s2_copy(q).wait_recv()
        return pall[q, z, c].astype(F32) + s1_recv[q, z].astype(F32) + s2_recv[q].astype(F32)

    def s3_copy(q):
        return rcopy(s3_send.at[q], s3_recv.at[y], s3_ss.at[q], s3_rs.at[y], ydev(q))

    def stage3(t):
        q = rem(y + off(t, NY), NY)
        s3_send[q] = total3(q).astype(BF)
        s3_copy(q).start()

    each(1, NY // 2 + 1, stage3)

    def b_wait(t):
        peer = rem(m + t, M)
        rcopy(wb.at[peer], rb.at[peer], b_ss.at[t - 1], b_rs.at[peer], sib).wait_recv()

    each(1, M, b_wait)
    rc[col] = jnp.sum(rb[...].astype(F32), axis=0)

    def col_peer(t):
        return ((x + off(rem(t, X) + 1, X)) % X) * ZH + rem(zh + off(div(t, X) + 1, ZH), ZH)

    def c_copy(t, slot):
        return rcopy(rc.at[slot], rc.at[slot], c_ss.at[t], c_rs.at[slot], (row, col_peer(t)))

    each(0, C - 1, lambda t: c_copy(t, col).start())
    each(NY // 2 + 1, NY, stage3)
    own[...] = total3(y)

    def collect(t):
        q = rem(y + t, NY)
        rcopy(s3_send.at[q], s3_recv.at[q], s3_ss.at[q], s3_rs.at[q], sib).wait_recv()
        own[...] += s3_recv[q].astype(F32)

    each(1, NY, collect)

    loads[4].wait()
    pulled = own[...] * scale
    p_hi = pulled.astype(BF)
    p_lo = (pulled - p_hi.astype(F32)).astype(BF)
    over_last = (((1,), (1,)), ((), ()))
    w = w_v[...]
    gf_ref[...] = lax.dot_general(p_hi, w, over_last, preferred_element_type=F32) + lax.dot_general(
        p_lo, w, over_last, preferred_element_type=F32
    )

    each(0, C - 1, lambda t: c_copy(t, col_peer(t)).wait_recv())
    wg_ref[c, m] = (jnp.sum(rc[...], axis=0) * norm).astype(BF)

    def d_copy(t, slot, core):
        return rcopy(wg_ref.at[c, slot], wg_ref.at[c, slot], d_ss.at[core, t], d_rs.at[c, slot], (row_peer(t) * 2 + core, col))

    def d_start(t):
        d_copy(t, m, 1 - c).start()

        @pl.when(t < M - 1)
        def _():
            d_copy(t, m, c).start()

    each(0, M, d_start)

    each(1, ZH, lambda t: to_z(t).wait_send())
    for k in range(ZH):
        each(1, X, lambda t: to_x(k, t).wait_send())
    each(1, NY, lambda t: f_to_y(t).wait_send())

    def drain(q):
        f_to_z(q).wait_send()
        s1_copy(q).wait_send()
        s2_copy(q).wait_send()

    each(0, NY, drain)
    each(1, NY, lambda t: s3_copy(rem(y + t, NY)).wait_send())
    a_copy.wait_send()
    each(0, M - 1, lambda t: b_copy(t).wait_send())
    each(0, C - 1, lambda t: c_copy(t, col).wait_send())

    def d_wait(t):
        d_copy(t, m, 1 - c).wait_send()
        rcopy(wg_ref.at[1 - c, t], wg_ref.at[1 - c, t], d_ss.at[0, t], d_rs.at[1 - c, t], sib).wait_recv()

        @pl.when(t < M - 1)
        def _():
            d_copy(t, m, c).wait_send()
            d_copy(t, row_peer(t), c).wait_recv()

    each(0, M, d_wait)


def finish(gf_in, wg_in, gf_out, wg_out):
    gf_out[...] = gf_in[...]
    wg_out[...] = wg_in[...].reshape(wg_out.shape).astype(F32)


def local(ZH, features, grad_out, relu_mask, degree, weight, adjacency, block_slot, block_count):
    R = lax.axis_size("row")
    C = lax.axis_size("col")
    n, width = features.shape
    entries, blk = adjacency.shape[2], adjacency.shape[3]
    NY, M, X = R // 4, R // 2, C // ZH
    part = (2, M, width // R, width)
    dma = pltpu.SemaphoreType.DMA
    vm = pltpu.VMEM
    vspec = pl.BlockSpec(memory_space=pltpu.VMEM)
    aspec = pl.BlockSpec(memory_space=pltpu.HBM)
    gf, wg = pl.pallas_call(
        functools.partial(kernel, R, C, ZH, float((n * R * C) ** -0.5)),
        out_shape=(
            jax.ShapeDtypeStruct((n, width), F32),
            jax.ShapeDtypeStruct(part, BF),
        ),
        in_specs=[aspec] * 8,
        out_specs=(vspec, vspec),
        scratch_shapes=[
            vm((n, width), BF),
            vm((n, width), BF),
            vm((n, width), jnp.int32),
            vm((1, n), jnp.int32),
            vm((width, width), BF),
            pltpu.SMEM((1, entries), jnp.int32),
            pltpu.SMEM((1, 1), jnp.int32),
            vm((entries + 1, blk, blk), BF),
            vm((NY, C * n, 2 * blk), BF),
            vm((8, 128), jnp.int32),
            pltpu.SMEM((8, 128), jnp.int32),
            vm((C, n, width), BF),
            vm((M, n, width), BF),
            vm((C // 2, width, 2 * n), BF),
            vm((NY, width, 2 * n), BF),
            vm((NY, 2, 2, n, width), BF),
            vm((NY, 2, n, width), BF),
            vm((NY, 2, n, width), BF),
            vm((NY, 2, n, width), BF),
            vm((NY, n, width), BF),
            vm((NY, n, width), BF),
            vm((NY, n, width), BF),
            vm((n, width), F32),
            vm(part, F32),
            vm(part[1:], F32),
            vm(part[1:], BF),
            vm(part[1:], BF),
            vm((C,) + part[2:], F32),
            dma((7,)), dma, dma,
            dma((ZH,)), dma((ZH, X)), dma((C,)),
            dma((NY,)), dma((NY,)), dma((M,)),
            dma((NY,)), dma((NY,)),
            dma((NY,)), dma((NY,)),
            dma((NY,)), dma((NY,)),
            dma, dma,
            dma((M,)), dma((M,)),
            dma((C,)), dma((C,)),
            dma((2, M)), dma((2, M)),
        ],
        compiler_params=pltpu.CompilerParams(
            collective_id=0, has_side_effects=True, vmem_limit_bytes=56 * 1024 * 1024
        ),
    )(
        features, grad_out, relu_mask, degree.reshape(1, n), weight,
        adjacency.reshape(entries, blk, blk), block_slot.reshape(1, entries), block_count,
    )
    return pl.pallas_call(
        finish,
        out_shape=(
            jax.ShapeDtypeStruct((n, width), F32),
            jax.ShapeDtypeStruct((width, width), F32),
        ),
        in_specs=[vspec, vspec],
        out_specs=(vspec, vspec),
    )(gf, wg)


def solution(mesh):
    placed = (
        P(("row", "col"), None),
        P(("row", "col"), None),
        P(("row", "col"), None),
        P(("row", "col")),
        P(),
        P("row", "col", None, None, None),
        P("row", "col", None),
        P("row", "col"),
    )
    inner = min(4, mesh.shape["col"])
    return jax.shard_map(
        functools.partial(local, inner),
        mesh=mesh, in_specs=placed, out_specs=(P(("row", "col"), None), P()), check_vma=False,
    )
```

```python
import functools

import jax
import jax.numpy as jnp
from jax import lax
from jax.experimental import pallas as pl
from jax.experimental.pallas import tpu as pltpu
from jax.sharding import PartitionSpec as P

MESH = pl.DeviceIdType.MESH
BF = jnp.bfloat16
F32 = jnp.float32
rem = lax.rem
div = lax.div


def kernel(
    R, C, ZH, norm,
    feat_hbm, gout_hbm, mask_hbm, deg_hbm, w_hbm, adj_hbm, slot_hbm, count_hbm,
    gf_ref, wg_ref,
    feat_v, gout_v, mask_v, deg_v, w_v, slot_ref, count_ref,
    adj_v, a_dense, inv_v, inv_s, gbuf, fbuf, gt, ft, pall,
    s1_recv, s_hi, s_lo, s2_recv, s3_send, s3_recv, own,
    wpart, ra, wb, rb, rc,
    in_sem, adj_sem, inv_sem, gz_ss, gx_ss, g_rs, fy_ss, fz_ss, f_rs,
    s1_ss, s1_rs, s2_ss, s2_rs, s3_ss, s3_rs,
    a_ss, a_rs, b_ss, b_rs, c_ss, c_rs, d_ss, d_rs,
):
    NY = R // 4
    M = R // 2
    X = C // ZH
    entries, blk = adj_hbm.shape[0], adj_hbm.shape[1]
    n, width = feat_hbm.shape
    row = lax.axis_index("row")
    col = lax.axis_index("col")
    y = div(row, 4)
    z = rem(div(row, 2), 2)
    c = rem(row, 2)
    m = div(row, 2)
    x = div(col, ZH)
    zh = rem(col, ZH)
    sib = (m * 2 + (1 - c), col)
    zdev = (y * 4 + (1 - z) * 2 + c, col)

    def ydev(k):
        return (k * 4 + z * 2 + c, col)

    def rcopy(src, dst, ss, rs, dev):
        return pltpu.make_async_remote_copy(
            src_ref=src, dst_ref=dst, send_sem=ss, recv_sem=rs,
            device_id=dev, device_id_type=MESH,
        )

    def each(lo, hi, body, unroll=1):
        def step(t, u):
            body(t)
            return u

        lax.fori_loop(lo, hi, step, 0, unroll=unroll)

    def off(t, size):
        return size // 2 + div(t, 2) * (2 * rem(t, 2) - 1)

    bar = pltpu.get_barrier_semaphore()

    def greet(dev):
        pl.semaphore_signal(bar, inc=1, device_id=dev, device_id_type=MESH)

    each(1, ZH, lambda t: greet((row, x * ZH + rem(zh + off(t, ZH), ZH))))
    each(1, NY, lambda t: greet(ydev(rem(y + off(t, NY), NY))))
    each(1, X, lambda t: greet((row, rem(x + off(t, X), X) * ZH + zh)))
    greet(zdev)
    greet(sib)

    loads = [
        pltpu.make_async_copy(s, d, in_sem.at[k])
        for k, (s, d) in enumerate(
            [(gout_hbm, gout_v), (mask_hbm, mask_v), (deg_hbm, deg_v), (feat_hbm, feat_v), (w_hbm, w_v),
             (slot_hbm, slot_ref), (count_hbm, count_ref)]
        )
    ]
    for copy in loads:
        copy.start()
    adj_copy = pltpu.make_async_copy(adj_hbm, adj_v.at[pl.ds(0, entries)], adj_sem)
    adj_copy.start()

    for copy in loads[:3]:
        copy.wait()
    scale_row = lax.rsqrt(deg_v[...].astype(F32))
    eye = lax.broadcasted_iota(jnp.int32, (n, n), 0) == lax.broadcasted_iota(jnp.int32, (n, n), 1)
    scale = jnp.sum(jnp.where(eye, jnp.broadcast_to(scale_row, (n, n)), 0.0), axis=1, keepdims=True)
    masked = gout_v[...].astype(F32) * mask_v[...].astype(F32)
    gbuf[col] = (masked * scale).astype(BF)
    loads[3].wait()
    fbuf[m] = (feat_v[...].astype(F32) * scale).astype(BF)

    pl.semaphore_wait(bar, ZH - 1 + X - 1 + NY - 1 + 2)

    def g_copy(slot, ss, dev):
        return rcopy(gbuf.at[slot], gbuf.at[slot], ss, g_rs.at[slot], dev)

    def f_copy(slot, ss, dev):
        return rcopy(fbuf.at[slot], fbuf.at[slot], ss, f_rs.at[slot], dev)

    def to_z(t):
        return g_copy(col, gz_ss.at[t], (row, x * ZH + rem(zh + t, ZH)))

    def to_x(k, t):
        return g_copy(x * ZH + rem(zh + k, ZH), gx_ss.at[k, t], (row, rem(x + t, X) * ZH + zh))

    def f_to_y(t):
        return f_copy(m, fy_ss.at[t], ydev(rem(y + t, NY)))

    def f_to_z(k):
        return f_copy(k * 2 + z, fz_ss.at[k], zdev)

    each(1, ZH, lambda t: to_z(off(t, ZH)).start())
    each(1, NY, lambda t: f_to_y(off(t, NY)).start())
    each(1, X, lambda t: to_x(0, off(t, X)).start())
    f_to_z(y).start()

    loads[5].wait()
    loads[6].wait()
    lane = lax.broadcasted_iota(jnp.int32, (8, 128), 1)
    live = count_ref[0, 0]

    def invert(b, acc):
        s = jnp.where(b < live, slot_ref[0, b], -1)
        return jnp.where(lane == s, b, acc)

    inv_v[...] = lax.fori_loop(0, entries, invert, jnp.full((8, 128), entries, jnp.int32))
    inv_copy = pltpu.make_async_copy(inv_v, inv_s, inv_sem)
    inv_copy.start()
    adj_v[entries] = jnp.zeros((blk, blk), BF)
    inv_copy.wait()
    adj_copy.wait()

    def fill(k):
        r = div(k, NY)
        q = rem(k, NY)
        for h in range(2):
            e = inv_s[0, r * (2 * NY) + q * 2 + h]
            a_dense[q, pl.ds(pl.multiple_of(r * blk, blk), blk), pl.ds(h * blk, blk)] = adj_v[e]

    each(0, C * n // blk * NY, fill)

    def forward_x(k):
        slot = x * ZH + rem(zh + k, ZH)
        g_copy(slot, gz_ss.at[k], sib).wait_recv()
        each(1, X, lambda t: to_x(k, off(t, X)).start())

    def forward_y(t):
        k = rem(y + t, NY)
        f_copy(k * 2 + z, fz_ss.at[k], sib).wait_recv()
        f_to_z(k).start()

    arrivals = [(2 * min(k, ZH - k), 0, k) for k in range(1, ZH)] + [(min(k, NY - k), 1, k) for k in range(1, NY)]
    each(1, ZH, lambda t: forward_x(off(ZH - t, ZH)))
    each(1, NY, lambda t: forward_y(off(NY - t, NY)))

    def wait_x(t):
        there = rem(x + t, X)

        @pl.when(t > 0)
        def _():
            for k in range(ZH):
                g_copy(there * ZH + k, gz_ss.at[0], sib).wait_recv()

        for k in range(ZH // 2):
            pair = there * (ZH // 2) + k
            gt[pair] = gbuf[pl.ds(2 * pair, 2)].reshape(2 * n, width).T

    each(0, X, wait_x)
    gtv = jnp.concatenate([gt[k] for k in range(C // 2)], axis=1)

    def s1_copy(q):
        return rcopy(pall.at[q, :, 1 - c], s1_recv.at[q], s1_ss.at[q], s1_rs.at[q], sib)

    def product(t):
        q = rem(y + off(t + 1, NY), NY)
        pt = jnp.dot(gtv, a_dense[q], preferred_element_type=F32).astype(BF)
        pall[q] = pt.T.reshape(2, 2, n, width)
        s1_copy(q).start()

    each(0, NY, product)

    each(0, NY, lambda k: f_copy(k * 2 + 1 - z, fz_ss.at[k], sib).wait_recv())

    def turn_f(k):
        ft[k] = fbuf[pl.ds(2 * k, 2)].reshape(2 * n, width).T

    each(0, NY, turn_f)

    def s2_copy(q):
        return rcopy(s_hi.at[q, 1 - z], s2_recv.at[q], s2_ss.at[q], s2_rs.at[q], zdev)

    def stage2(t):
        q = rem(y + off(t + 1, NY), NY)
        s1_copy(q).wait_recv()
        both = pall[q, :, c].astype(F32) + s1_recv[q].astype(F32)
        hi = both.astype(BF)
        s_hi[q] = hi
        s_lo[q] = (both - hi.astype(F32)).astype(BF)
        s2_copy(q).start()

    each(0, NY, stage2)
    ftv = jnp.concatenate([ft[k] for k in range(NY)], axis=1)
    wt = jnp.dot(ftv, s_hi[...].reshape(M * n, width), preferred_element_type=F32)
    wt = wt + jnp.dot(ftv, s_lo[...].reshape(M * n, width), preferred_element_type=F32)
    wpart[...] = wt.reshape(wpart.shape)
    a_copy = rcopy(wpart.at[1 - c], ra, a_ss, a_rs, sib)
    a_copy.start()

    a_copy.wait_recv()
    wb[...] = (wpart[c] + ra[...]).astype(BF)

    def row_peer(t):
        return (rem(y + off(div(t, 2) + 1, NY), NY)) * 2 + rem(z + 1 - rem(t, 2), 2)

    def b_copy(t):
        peer = row_peer(t)
        return rcopy(wb.at[peer], rb.at[m], b_ss.at[t], b_rs.at[m], (peer * 2 + c, col))

    each(0, M - 1, lambda t: b_copy(t).start())
    rb[m] = wb[m]

    def total3(q):
        s2_copy(q).wait_recv()
        return pall[q, z, c].astype(F32) + s1_recv[q, z].astype(F32) + s2_recv[q].astype(F32)

    def s3_copy(q):
        return rcopy(s3_send.at[q], s3_recv.at[y], s3_ss.at[q], s3_rs.at[y], ydev(q))

    def stage3(t):
        q = rem(y + off(t, NY), NY)
        s3_send[q] = total3(q).astype(BF)
        s3_copy(q).start()

    each(1, NY // 4 + 1, stage3)

    def b_wait(t):
        peer = rem(m + t, M)
        rcopy(wb.at[peer], rb.at[peer], b_ss.at[t - 1], b_rs.at[peer], sib).wait_recv()

    each(1, M, b_wait)
    rc[col] = jnp.sum(rb[...].astype(F32), axis=0)

    def col_peer(t):
        return ((x + off(rem(t, X) + 1, X)) % X) * ZH + rem(zh + off(div(t, X) + 1, ZH), ZH)

    def c_copy(t, slot):
        return rcopy(rc.at[slot], rc.at[slot], c_ss.at[t], c_rs.at[slot], (row, col_peer(t)))

    each(0, C - 1, lambda t: c_copy(t, col).start())
    each(NY // 4 + 1, NY, stage3)
    own[...] = total3(y)

    def collect(t):
        q = rem(y + t, NY)
        rcopy(s3_send.at[q], s3_recv.at[q], s3_ss.at[q], s3_rs.at[q], sib).wait_recv()
        own[...] += s3_recv[q].astype(F32)

    each(1, NY, collect)

    loads[4].wait()
    pulled = own[...] * scale
    p_hi = pulled.astype(BF)
    p_lo = (pulled - p_hi.astype(F32)).astype(BF)
    over_last = (((1,), (1,)), ((), ()))
    w = w_v[...]
    gf_ref[...] = lax.dot_general(p_hi, w, over_last, preferred_element_type=F32) + lax.dot_general(
        p_lo, w, over_last, preferred_element_type=F32
    )

    each(0, C - 1, lambda t: c_copy(t, col_peer(t)).wait_recv())
    wg_ref[c, m] = (jnp.sum(rc[...], axis=0) * norm).astype(BF)

    def d_copy(t, slot, core):
        return rcopy(wg_ref.at[c, slot], wg_ref.at[c, slot], d_ss.at[core, t], d_rs.at[c, slot], (row_peer(t) * 2 + core, col))

    def d_start(t):
        d_copy(t, m, 1 - c).start()

        @pl.when(t < M - 1)
        def _():
            d_copy(t, m, c).start()

    each(0, M, d_start)

    each(1, ZH, lambda t: to_z(t).wait_send())
    for k in range(ZH):
        each(1, X, lambda t: to_x(k, t).wait_send())
    each(1, NY, lambda t: f_to_y(t).wait_send())

    def drain(q):
        f_to_z(q).wait_send()
        s1_copy(q).wait_send()
        s2_copy(q).wait_send()

    each(0, NY, drain)
    each(1, NY, lambda t: s3_copy(rem(y + t, NY)).wait_send())
    a_copy.wait_send()
    each(0, M - 1, lambda t: b_copy(t).wait_send())
    each(0, C - 1, lambda t: c_copy(t, col).wait_send())

    def d_wait(t):
        d_copy(t, m, 1 - c).wait_send()
        rcopy(wg_ref.at[1 - c, t], wg_ref.at[1 - c, t], d_ss.at[0, t], d_rs.at[1 - c, t], sib).wait_recv()

        @pl.when(t < M - 1)
        def _():
            d_copy(t, m, c).wait_send()
            d_copy(t, row_peer(t), c).wait_recv()

    each(0, M, d_wait)


def finish(gf_in, wg_in, gf_out, wg_out):
    gf_out[...] = gf_in[...]
    wg_out[...] = wg_in[...].reshape(wg_out.shape).astype(F32)


def local(ZH, features, grad_out, relu_mask, degree, weight, adjacency, block_slot, block_count):
    R = lax.axis_size("row")
    C = lax.axis_size("col")
    n, width = features.shape
    entries, blk = adjacency.shape[2], adjacency.shape[3]
    NY, M, X = R // 4, R // 2, C // ZH
    part = (2, M, width // R, width)
    dma = pltpu.SemaphoreType.DMA
    vm = pltpu.VMEM
    vspec = pl.BlockSpec(memory_space=pltpu.VMEM)
    aspec = pl.BlockSpec(memory_space=pltpu.HBM)
    gf, wg = pl.pallas_call(
        functools.partial(kernel, R, C, ZH, float((n * R * C) ** -0.5)),
        out_shape=(
            jax.ShapeDtypeStruct((n, width), F32),
            jax.ShapeDtypeStruct(part, BF),
        ),
        in_specs=[aspec] * 8,
        out_specs=(vspec, vspec),
        scratch_shapes=[
            vm((n, width), BF),
            vm((n, width), BF),
            vm((n, width), jnp.int32),
            vm((1, n), jnp.int32),
            vm((width, width), BF),
            pltpu.SMEM((1, entries), jnp.int32),
            pltpu.SMEM((1, 1), jnp.int32),
            vm((entries + 1, blk, blk), BF),
            vm((NY, C * n, 2 * blk), BF),
            vm((8, 128), jnp.int32),
            pltpu.SMEM((8, 128), jnp.int32),
            vm((C, n, width), BF),
            vm((M, n, width), BF),
            vm((C // 2, width, 2 * n), BF),
            vm((NY, width, 2 * n), BF),
            vm((NY, 2, 2, n, width), BF),
            vm((NY, 2, n, width), BF),
            vm((NY, 2, n, width), BF),
            vm((NY, 2, n, width), BF),
            vm((NY, n, width), BF),
            vm((NY, n, width), BF),
            vm((NY, n, width), BF),
            vm((n, width), F32),
            vm(part, F32),
            vm(part[1:], F32),
            vm(part[1:], BF),
            vm(part[1:], BF),
            vm((C,) + part[2:], F32),
            dma((7,)), dma, dma,
            dma((ZH,)), dma((ZH, X)), dma((C,)),
            dma((NY,)), dma((NY,)), dma((M,)),
            dma((NY,)), dma((NY,)),
            dma((NY,)), dma((NY,)),
            dma((NY,)), dma((NY,)),
            dma, dma,
            dma((M,)), dma((M,)),
            dma((C,)), dma((C,)),
            dma((2, M)), dma((2, M)),
        ],
        compiler_params=pltpu.CompilerParams(
            collective_id=0, has_side_effects=True, vmem_limit_bytes=56 * 1024 * 1024
        ),
    )(
        features, grad_out, relu_mask, degree.reshape(1, n), weight,
        adjacency.reshape(entries, blk, blk), block_slot.reshape(1, entries), block_count,
    )
    return pl.pallas_call(
        finish,
        out_shape=(
            jax.ShapeDtypeStruct((n, width), F32),
            jax.ShapeDtypeStruct((width, width), F32),
        ),
        in_specs=[vspec, vspec],
        out_specs=(vspec, vspec),
    )(gf, wg)


def solution(mesh):
    placed = (
        P(("row", "col"), None),
        P(("row", "col"), None),
        P(("row", "col"), None),
        P(("row", "col")),
        P(),
        P("row", "col", None, None, None),
        P("row", "col", None),
        P("row", "col"),
    )
    inner = min(4, mesh.shape["col"])
    return jax.shard_map(
        functools.partial(local, inner),
        mesh=mesh, in_specs=placed, out_specs=(P(("row", "col"), None), P()), check_vma=False,
    )
```
